256 devices in a mesh: row: 32 (over x, z_lo, core), col: 8 (over z_hi, y).
Axes of the slice: x: 4, y: 4, z: 8 (z_hi: 2, z_lo: 4; z = z_hi * 4 + z_lo), core: 2. Of those that a mesh axis runs over, the one named last changes fastest.
Arguments:
- forcing: float32 [32, 8, 96, 2048], P('row', 'col'), may hold values from -4 to 4
- local_op: bfloat16 [32, 8, 2048, 2048], P('row', 'col'), may hold values from -0.027621359 to 1.0376214
- material: int32 [32, 8, 2048], P('row', 'col'), may hold values from 0 to 7
- stiffness: float32 [8], replicated, may hold values from 0.25 to 4
Outputs:
- preconditioned: float32 [32, 8, 96, 2048], P('row', 'col')
- residual: float32 [32, 8, 96, 2048], P('row', 'col')
The draws below stay inside these ranges and needn't reach their ends.
All inputs are finite; a program needn't handle non-finite values.
Results may differ from the reference program's by a relative error of at most 0.007.
Values may be sent and summed in bfloat16 or wider, within the bound.
No kernel may reach another device: no remote copies, remote signals or barrier semaphores. Data moves between devices by JAX's collectives and lax.ppermute only.
A program may use at most 64 MiB of HBM per device.

```python
import math
import jax
import jax.numpy as jnp
from jax import lax

ORDER = 2048
LOADS = 96
CLASSES = 8
N_ROW = 32
N_COL = 8


def draw_local_op(key, part):
    side_width = ORDER // 4
    first_key, second_key = jax.random.split(jax.random.fold_in(key, 11))
    noise = jnp.clip(jax.random.normal(first_key, (N_ROW, N_COL, ORDER, ORDER), jnp.float32), -6.0, 6.0) * (0.2 / math.sqrt(ORDER))
    strength = jax.random.uniform(second_key, (N_ROW, N_COL, ORDER, 1), jnp.float32, math.log(0.3), math.log(30.0))
    carried = jnp.exp(-jnp.exp(strength) / (N_ROW + N_COL))
    incoming = jnp.arange(ORDER, dtype=jnp.int32)[:, None]
    outgoing = jnp.arange(ORDER, dtype=jnp.int32)[None, :]
    side_index = incoming // side_width
    opposite = (side_index + 1 - 2 * (side_index % 2)) * side_width + incoming % side_width
    identity = (incoming == outgoing).astype(jnp.float32)
    crossing = (outgoing == opposite).astype(jnp.float32)
    return (noise + 0.3 * identity + carried * crossing).astype(jnp.bfloat16)


def plant(entries, rng, smallest, largest):
    longest = entries.shape.index(max(entries.shape))
    spots = []
    for shift in (0, 1):
        where = [jax.random.randint(jax.random.fold_in(rng, axis), (), 0, length) for axis, length in enumerate(entries.shape)]
        where[longest] = (where[longest] + shift) % entries.shape[longest]
        spots.append(tuple(where))
    return entries.at[spots[0]].set(smallest).at[spots[1]].set(largest)


def shard_levels(own_key, extent, cuts, least, high):
    factor_of, own = 1.0, jax.random.fold_in(own_key, 6)
    for dim, blocks in cuts:
        draws = jnp.exp(jax.random.uniform(jax.random.fold_in(own, dim), (blocks,), jnp.float32, least / len(cuts), high / len(cuts)))
        factor_of = factor_of * jnp.repeat(draws, extent[dim] // blocks).reshape([-1 if axis == dim else 1 for axis in range(len(extent))])
    return factor_of


def bell_draw(key, dims, width, most, pieces=(), kind=jnp.bfloat16):
    level = shard_levels(key, dims, pieces, -0.22, 0.18) if pieces else 1.0
    entries = jax.random.normal(key, dims, jnp.float32) * width * level
    return jnp.minimum(jnp.maximum(entries, -most), most).astype(kind)


def setup_inputs(seed: int = 0) -> dict:
    seeds = jax.random.split(jax.random.key(seed), 5)
    forcing = bell_draw(seeds[0], (N_ROW, N_COL, LOADS, ORDER), 0.5, 4.0, ((0, 32), (1, 8)), jnp.float32)
    local_op = draw_local_op(jax.random.fold_in(seeds[4], 71), 0)
    material = plant(jax.random.randint(seeds[2], (N_ROW, N_COL, ORDER), 0, CLASSES), jax.random.fold_in(seeds[2], 1), 0, CLASSES - 1).astype(jnp.int32)
    stiffness = jnp.clip(jnp.exp(jax.random.uniform(seeds[3], (CLASSES,), jnp.float32, math.log(0.25), math.log(4.0))), 0.25, 4.0)
    return dict(forcing=forcing, local_op=local_op, material=material, stiffness=stiffness)


def side_block(values, side_index):
    side_width = values.shape[-1] // 4
    return values[..., side_index * side_width:(side_index + 1) * side_width]


def sweep_grid(forcing, local_op, forward_rows, forward_cols):
    side_width = ORDER // 4
    in_row, out_row = (0, 1) if forward_rows else (1, 0)
    in_col, out_col = (2, 3) if forward_cols else (3, 2)

    def cell_step(col_trace, inputs):
        source, matrix, row_trace = inputs
        solved = jnp.dot(source.astype(jnp.bfloat16), matrix, preferred_element_type=jnp.float32)
        solved = solved + jnp.dot(row_trace, matrix[in_row * side_width:(in_row + 1) * side_width], preferred_element_type=jnp.float32)
        solved = solved + jnp.dot(col_trace, matrix[in_col * side_width:(in_col + 1) * side_width], preferred_element_type=jnp.float32)
        next_col = side_block(solved, out_col).astype(jnp.bfloat16)
        next_row = side_block(solved, out_row).astype(jnp.bfloat16)
        return next_col, (solved, next_row)

    def row_step(row_traces, inputs):
        source_row, matrix_row = inputs
        starting = jnp.zeros((LOADS, side_width), jnp.bfloat16)
        unused, (solved_row, next_traces) = lax.scan(cell_step, starting, (source_row, matrix_row, row_traces), reverse=not forward_cols)
        return next_traces, solved_row

    initial = jnp.zeros((N_COL, LOADS, side_width), jnp.bfloat16)
    unused, solved = lax.scan(row_step, initial, (forcing, local_op), reverse=not forward_rows)
    return solved


def reference(forcing, local_op, material, stiffness):
    summed = jnp.zeros(forcing.shape, jnp.float32)
    for forward_rows in (True, False):
        for forward_cols in (True, False):
            summed = summed + sweep_grid(forcing, local_op, forward_rows, forward_cols)
    preconditioned = summed * 0.25
    rounded = lax.optimization_barrier(preconditioned.astype(jnp.bfloat16)).astype(jnp.float32)
    zero_row = jnp.zeros_like(side_block(rounded, 0)[:1])
    zero_col = jnp.zeros_like(side_block(rounded, 0)[:, :1])
    from_above = jnp.concatenate([zero_row, side_block(rounded, 1)[:-1]], axis=0)
    from_below = jnp.concatenate([side_block(rounded, 0)[1:], zero_row], axis=0)
    from_left = jnp.concatenate([zero_col, side_block(rounded, 3)[:, :-1]], axis=1)
    from_right = jnp.concatenate([side_block(rounded, 2)[:, 1:], zero_col], axis=1)
    facing = jnp.concatenate([from_above, from_below, from_left, from_right], axis=-1)
    classes = jnp.arange(CLASSES, dtype=jnp.int32)
    coupling = jnp.sum(jnp.where(material[..., None] == classes, stiffness, 0.0), axis=-1)
    residual = forcing - preconditioned + coupling[:, :, None, :] * (facing - preconditioned)
    return preconditioned, residual
```

```python
import functools

import jax
import jax.numpy as jnp
from jax import lax
from jax.experimental import pallas as pl
from jax.experimental.pallas import tpu as pltpu
from jax.sharding import PartitionSpec as P


BF16 = jnp.bfloat16
F32 = jnp.float32
AXES = ("row", "col")
MERGED = 7


def coords(device, n_col):
    row, col = divmod(device, n_col)
    return (row // 8, col % 4, (col // 4) * 4 + (row // 2) % 4, row % 2)


def distance(a, b, n_col):
    pa, pb = coords(a, n_col), coords(b, n_col)
    total = 0
    for u, v, size in zip(pa, pb, (4, 4, 8)):
        gap = abs(u - v)
        total += min(gap, size - gap)
    return 2 * total + (pa[3] != pb[3])


def completed(pairs, n_row, n_col):
    count = n_row * n_col
    sources = {a for a, _ in pairs}
    free = set(range(count)) - {b for _, b in pairs}
    out = list(pairs)
    left = []
    for device in range(count):
        if device in sources:
            continue
        row, col = divmod(device, n_col)
        partner = (row ^ 1) * n_col + col
        if partner in free:
            out.append((device, partner))
            free.discard(partner)
        else:
            left.append(device)
    for place, device in enumerate(left):
        rest = left[place + 1 :]
        choices = [b for b in sorted(free) if b != device]
        if len(rest) == 1:
            choices = [b for b in choices if free - {b} != {rest[0]}]
        best = min(choices, key=lambda b: distance(device, b, n_col))
        out.append((device, best))
        free.discard(best)
    assert len({a for a, _ in out}) == count and len({b for _, b in out}) == count
    assert all(a != b for a, b in out)
    return tuple(sorted(out))


def tick_pairs(n_row, n_col):
    chips = n_row // 2
    ticks = chips + n_col - 1
    rows = [[] for _ in range(ticks)]
    cols = [[] for _ in range(ticks)]
    for chip in range(chips):
        for core in range(2):
            for col in range(n_col):
                for step in (1, -1):
                    place = chip if core == 0 else chips - 1 - chip
                    place += col if step > 0 else n_col - 1 - col
                    here = (2 * chip + core) * n_col + col
                    onward = chip + 1 - 2 * core
                    if 0 <= onward < chips:
                        rows[place].append((here, (2 * onward + core) * n_col + col))
                    if 0 <= col + step < n_col:
                        cols[place].append((here, (2 * chip + core) * n_col + col + step))
    return rows[:-1], cols[:-1]


def patterns(pairs, n_row, n_col):
    steps = len(pairs)
    half = steps // 2
    result = [None] * steps
    for t in range(half):
        if t < MERGED:
            both = completed(pairs[t] + pairs[t + half], n_row, n_col)
            result[t] = result[t + half] = both
    for t in range(steps):
        if result[t] is None:
            result[t] = completed(pairs[t], n_row, n_col)
    return result


def swaps(n_row, n_col):
    chip, off, even, odd = [], [], [], []
    for row in range(n_row):
        for col in range(n_col):
            here = row * n_col + col
            chip.append((here, (row ^ 1) * n_col + col))
            other = row + 1 if row % 2 else row - 1
            if 0 <= other < n_row:
                off.append((here, other * n_col + col))
            else:
                off.append((here, row * n_col + (col ^ 1)))
            even.append((here, row * n_col + (col ^ 1)))
            side = col + 1 if col % 2 else col - 1
            if 0 <= side < n_col:
                odd.append((here, row * n_col + side))
            else:
                odd.append((here, (row ^ 1) * n_col + col))
    return chip, off, even, odd


def whole(count):
    return [pl.BlockSpec(memory_space=pltpu.VMEM)] * count


def call(kernel, inputs, outputs, cost, specs=None, scratch=(), aliases=None, limit=16 << 20):
    return pl.pallas_call(
        kernel,
        out_shape=outputs,
        in_specs=specs or whole(len(inputs)),
        out_specs=jax.tree.map(lambda _: pl.BlockSpec(memory_space=pltpu.VMEM), outputs),
        scratch_shapes=list(scratch),
        input_output_aliases=aliases or {},
        cost_estimate=pl.CostEstimate(flops=cost, bytes_accessed=1 << 16, transcendentals=0),
        compiler_params=pltpu.CompilerParams(vmem_limit_bytes=limit),
    )(*inputs)


def dot(a, b):
    return jnp.dot(a, b, preferred_element_type=F32)


def span(index, width):
    if isinstance(index, int):
        return pl.ds(index * width, width)
    return pl.ds(pl.multiple_of(index * width, width), width)


def gather_kernel(side, op_ref, out_ref, sems):
    core = lax.rem(lax.axis_index("row"), 2)
    into, out = 1 - core, core
    blocks = [(into, out)]
    blocks += [(into, 3 - h) for h in range(2)]
    blocks += [(2 + h, out) for h in range(2)]
    blocks += [(2 + h, 3 - h) for h in range(2)]
    copies = []
    for n, (a, b) in enumerate(blocks):
        copies.append(
            pltpu.make_async_copy(
                op_ref.at[0, 0, span(a, side), span(b, side)], out_ref.at[n], sems.at[n]
            )
        )
    for copy in copies:
        copy.start()
    for copy in copies:
        copy.wait()


def base_kernel(chunk, forcing_ref, op_ref, held_ref, base_ref, send_ref, half_ref, sems):
    order = held_ref.shape[0]
    side = order // 4
    steps = order // chunk
    core = lax.rem(lax.axis_index("row"), 2)
    copies = [
        pltpu.make_async_copy(
            op_ref.at[0, 0, pl.ds(n * chunk, chunk), :],
            held_ref.at[pl.ds(n * chunk, chunk), :],
            sems.at[n],
        )
        for n in range(steps)
    ]
    for copy in copies:
        copy.start()
    half_ref[...] = forcing_ref[0, 0].astype(BF16)
    for n in range(steps):
        copies[n].wait()
        part = dot(half_ref[:, n * chunk : (n + 1) * chunk], held_ref[pl.ds(n * chunk, chunk), :])
        if n == 0:
            base_ref[...] = part
        else:
            base_ref[...] += part
    send_ref[:, :side] = base_ref[:, span(core, side)]
    send_ref[:, side:] = base_ref[:, 2 * side :]


def place(t, n_row, n_col):
    row, col = lax.axis_index("row"), lax.axis_index("col")
    core, chip = lax.rem(row, 2), lax.div(row, 2)
    last = n_row // 2 - 1
    down = jnp.where(core == 0, chip, last - chip)
    first = down + col == t
    second = down + n_col - 1 - col == t
    head = jnp.where(second, 1, 0)
    row_edge = down == 0
    col_edge = jnp.where(second, col == n_col - 1, col == 0)
    return core, head, jnp.logical_or(first, second), row_edge, col_edge


def unless(edge, value):
    return jnp.where(edge, jnp.zeros_like(value), value)


def row_kernel(t, n_row, n_col, row_ref, col_ref, held_ref, near_ref, base_ref, far_ref, mid_ref, out_ref):
    core, head, active, row_edge, col_edge = place(t, n_row, n_col)
    loads, side = row_ref.shape

    @pl.when(active)
    def _():
        out = 1 - core
        row_in = unless(row_edge, row_ref[...])
        own = unless(col_edge, col_ref[:loads])
        value = base_ref[:, span(out, side)]
        value += dot(row_in, held_ref[span(core, side), span(out, side)])
        value += dot(own, held_ref[span(2 + head, side), span(out, side)])
        mid_ref[...] = value.astype(BF16)
        other = unless(col_edge, col_ref[loads:])
        value = far_ref[:, :side]
        value += dot(other, near_ref[3 + head])
        value += dot(mid_ref[...], near_ref[0])
        out_ref[...] = value.astype(BF16)


def col_kernel(
    t, n_row, n_col, row_ref, col_ref, mid_ref, held_ref, near_ref, base_ref, far_base_ref, *refs
):
    out_ref, own_ref, far_ref = refs[-3:]
    core, head, active, row_edge, col_edge = place(t, n_row, n_col)
    loads, side = row_ref.shape

    @pl.when(active)
    def _():
        out = 3 - head
        row_in = unless(row_edge, row_ref[...])
        own = unless(col_edge, col_ref[:loads])
        value = base_ref[:, span(out, side)]
        value += dot(row_in, held_ref[span(core, side), span(out, side)])
        value += dot(own, held_ref[span(2 + head, side), span(out, side)])
        out_ref[:loads] = value.astype(BF16)
        other = unless(col_edge, col_ref[loads:])
        value = far_base_ref[:, span(2 - head, side)]
        value += dot(mid_ref[...], near_ref[1 + head])
        value += dot(other, near_ref[5 + head])
        out_ref[loads:] = value.astype(BF16)
        own_ref[2 * head] = row_in
        own_ref[2 * head + 1] = own
        far_ref[2 * head] = mid_ref[...]
        far_ref[2 * head + 1] = other


def last_kernel(t, n_row, n_col, row_ref, col_ref, held_ref, base_ref, old_own, old_far, own_ref, far_ref):
    core, head, active, row_edge, col_edge = place(t, n_row, n_col)
    loads, side = row_ref.shape

    @pl.when(active)
    def _():
        out = 1 - core
        row_in = unless(row_edge, row_ref[...])
        own = unless(col_edge, col_ref[:loads])
        other = unless(col_edge, col_ref[loads:])
        value = base_ref[:, span(out, side)]
        value += dot(row_in, held_ref[span(core, side), span(out, side)])
        value += dot(own, held_ref[span(2 + head, side), span(out, side)])
        own_ref[2 * head] = row_in
        own_ref[2 * head + 1] = own
        far_ref[2 * head] = value.astype(BF16)
        far_ref[2 * head + 1] = other


def sum_kernel(own_ref, other_ref, held_ref, base_ref, out_ref, chip_ref, off_ref, even_ref, odd_ref, left_ref):
    core = lax.rem(lax.axis_index("row"), 2)
    parity = lax.rem(lax.axis_index("col"), 2)
    side = own_ref.shape[-1]

    def wide(ref, n):
        return ref[n].astype(F32)

    left_ref[:, span(core, side)] = ((wide(own_ref, 0) + wide(own_ref, 2)) * 0.25).astype(BF16)
    left_ref[:, span(1 - core, side)] = (
        (wide(other_ref, 0) + wide(other_ref, 2)) * 0.25
    ).astype(BF16)
    for h in range(2):
        both = wide(own_ref, 2 * h + 1) + wide(other_ref, 2 * h + 1)
        left_ref[:, span(2 + h, side)] = (both * 0.25).astype(BF16)
    for n in range(4):
        out_ref[:, span(n, side)] = base_ref[:, span(n, side)] + dot(
            left_ref[...], held_ref[:, span(n, side)]
        )
    chip_ref[...] = out_ref[:, span(1 - core, side)].astype(BF16)
    off_ref[...] = out_ref[:, span(core, side)].astype(BF16)
    even_ref[...] = out_ref[:, span(3 - parity, side)].astype(BF16)
    odd_ref[...] = out_ref[:, span(2 + parity, side)].astype(BF16)


def residual_kernel(n_row, n_col, forcing_ref, pre_ref, coupling_ref, chip_ref, off_ref, even_ref, odd_ref, pre_out, out_ref):
    row, col = lax.axis_index("row"), lax.axis_index("col")
    core, parity = lax.rem(row, 2), lax.rem(col, 2)
    side = chip_ref.shape[-1]

    def finish(index, facing):
        block = span(index, side)
        pre = pre_ref[:, block]
        pre_out[0, 0, :, block] = pre
        out_ref[0, 0, :, block] = (
            forcing_ref[0, 0, :, block] - pre + coupling_ref[:, block] * (facing - pre)
        )

    row_end = jnp.logical_or(row == 0, row == n_row - 1)
    col_end = jnp.logical_or(col == 0, col == n_col - 1)
    finish(1 - core, chip_ref[...].astype(F32))
    finish(core, unless(row_end, off_ref[...].astype(F32)))
    finish(3 - parity, even_ref[...].astype(F32))
    finish(2 + parity, unless(col_end, odd_ref[...].astype(F32)))


def local(n_row, n_col, forcing, local_op, material, stiffness):
    loads, order = forcing.shape[2:]
    side = order // 4
    chunk = side
    chip_swap, off_swap, even_swap, odd_swap = swaps(n_row, n_col)
    row_pairs, col_pairs = tick_pairs(n_row, n_col)
    row_sets = patterns(row_pairs, n_row, n_col)
    col_sets = patterns(col_pairs, n_row, n_col)

    def vmem(shape, dtype):
        return pltpu.VMEM(shape, dtype)

    def shift(value, pairs):
        return lax.ppermute(value, AXES, pairs)

    anywhere = pl.BlockSpec(memory_space=pltpu.HBM)
    local_op = pltpu.with_memory_space_constraint(local_op, pltpu.HBM)
    parcel = call(
        functools.partial(gather_kernel, side),
        (local_op,),
        vmem((7, side, side), BF16),
        1 << 20,
        specs=[anywhere],
        scratch=[pltpu.SemaphoreType.DMA((7,))],
    )
    near = shift(parcel, chip_swap)
    held, base, base_parcel = call(
        functools.partial(base_kernel, chunk),
        (forcing, local_op),
        (
            vmem((order, order), BF16),
            vmem((loads, order), F32),
            vmem((loads, 3 * side), F32),
        ),
        2 * loads * order * order,
        specs=[pl.BlockSpec(memory_space=pltpu.VMEM), anywhere],
        scratch=[pltpu.VMEM((loads, order), BF16), pltpu.SemaphoreType.DMA((order // chunk,))],
    )
    far = shift(base_parcel, chip_swap)
    classes = jnp.arange(stiffness.shape[0], dtype=jnp.int32)
    coupling = jnp.sum(
        jnp.where(material[0, 0][None, :] == classes[:, None], stiffness[:, None], 0.0), axis=0
    )[None, :]

    row_in = jnp.zeros((loads, side), BF16)
    col_in = jnp.zeros((2 * loads, side), BF16)
    kept = ()
    steps = len(row_sets)
    work = 8 * loads * side * side
    traces = (vmem((4, loads, side), BF16),) * 2
    for t in range(steps):
        mid, row_out = call(
            functools.partial(row_kernel, t, n_row, n_col),
            (row_in, col_in, held, near, base, far),
            (vmem((loads, side), BF16), vmem((loads, side), BF16)),
            work,
        )
        row_next = shift(row_out, row_sets[t])
        col_out, *kept = call(
            functools.partial(col_kernel, t, n_row, n_col),
            (row_in, col_in, mid, held, near, base, far, *kept),
            (vmem((2 * loads, side), BF16), *traces),
            work,
            aliases={7: 1, 8: 2} if kept else None,
        )
        col_next = shift(col_out, col_sets[t])
        row_in, col_in = row_next, col_next
    own, away = call(
        functools.partial(last_kernel, steps, n_row, n_col),
        (row_in, col_in, held, base, *kept),
        traces,
        work,
        aliases={4: 0, 5: 1},
    )
    other = shift(away, chip_swap)
    trace = vmem((loads, side), BF16)
    pre, chip, off, even, odd = call(
        sum_kernel,
        (own, other, held, base),
        (vmem((loads, order), F32), trace, trace, trace, trace),
        2 * loads * order * order,
        scratch=[pltpu.VMEM((loads, order), BF16)],
    )
    arrived = (
        shift(chip, chip_swap),
        shift(off, off_swap),
        shift(even, even_swap),
        shift(odd, odd_swap),
    )
    shape = jax.ShapeDtypeStruct((1, 1, loads, order), F32)
    return tuple(
        call(
            functools.partial(residual_kernel, n_row, n_col),
            (forcing, pre, coupling, *arrived),
            (shape, shape),
            1 << 20,
        )
    )


def solution(mesh):
    n_row, n_col = mesh.shape["row"], mesh.shape["col"]
    return jax.shard_map(
        functools.partial(local, n_row, n_col),
        mesh=mesh,
        in_specs=(
            P("row", "col", None, None),
            P("row", "col", None, None),
            P("row", "col", None),
            P(),
        ),
        out_specs=(P("row", "col", None, None), P("row", "col", None, None)),
        check_vma=False,
    )
```

```python
import functools

import jax
import jax.numpy as jnp
from jax import lax
from jax.experimental import pallas as pl
from jax.experimental.pallas import tpu as pltpu
from jax.sharding import PartitionSpec as P


BF16 = jnp.bfloat16
F32 = jnp.float32
AXES = ("row", "col")
GROUPS = (
    (0, 21,),
    (1, 20,),
    (2, 19,),
    (3, 18,),
    (4, 17,),
    (5, 16,),
    (6, 15,),
    (7,),
    (8,),
    (9,),
    (10,),
    (11,),
    (12,),
    (13,),
    (14,),
)
ROW_FILL = (
    (
        16, 53, 10, 11, 12, 13, 78, 23, 201, 1, 2, 3, 4, 5, 6, 7,
        24, 25, 26, 27, 28, 29, 30, 31, 8, 17, 18, 19, 20, 21, 22, 15,
        40, 41, 42, 43, 44, 45, 46, 47, 32, 33, 34, 35, 36, 37, 38, 39,
        56, 241, 58, 59, 60, 73, 246, 63, 48, 197, 70, 51, 52, 9, 54, 55,
        72, 193, 74, 75, 76, 77, 50, 79, 64, 65, 66, 67, 68, 69, 14, 71,
        88, 89, 90, 91, 92, 93, 94, 95, 80, 81, 82, 83, 84, 85, 86, 87,
        104, 105, 106, 107, 108, 109, 110, 111, 96, 97, 98, 99, 100, 101, 102, 103,
        120, 121, 122, 123, 124, 125, 126, 127, 112, 113, 114, 115, 116, 117, 118, 119,
        136, 137, 138, 139, 140, 141, 142, 143, 128, 129, 130, 131, 132, 133, 134, 135,
        152, 153, 154, 155, 156, 157, 158, 159, 144, 145, 146, 147, 148, 149, 150, 151,
        168, 169, 170, 171, 172, 173, 174, 175, 160, 161, 162, 163, 164, 165, 166, 167,
        184, 205, 186, 187, 188, 189, 62, 191, 176, 57, 178, 179, 180, 181, 182, 183,
        200, 61, 202, 203, 204, 177, 206, 207, 192, 0, 194, 195, 196, 49, 198, 199,
        216, 217, 218, 219, 220, 221, 222, 223, 208, 209, 210, 211, 212, 213, 214, 215,
        240, 233, 234, 235, 236, 237, 238, 247, 224, 225, 226, 227, 228, 229, 230, 231,
        248, 249, 250, 251, 252, 253, 254, 255, 232, 185, 242, 243, 244, 245, 190, 239,
    ),
    (
        8, 17, 10, 52, 48, 13, 22, 15, 0, 1, 98, 3, 4, 140, 6, 7,
        32, 121, 108, 27, 28, 29, 213, 39, 16, 9, 18, 19, 20, 253, 14, 23,
        40, 41, 42, 43, 47, 45, 46, 26, 24, 33, 34, 44, 36, 37, 38, 31,
        56, 57, 58, 59, 60, 61, 62, 63, 176, 49, 50, 51, 80, 53, 54, 55,
        72, 73, 74, 75, 76, 242, 182, 79, 64, 65, 66, 11, 68, 69, 70, 71,
        88, 89, 90, 91, 92, 93, 94, 95, 163, 250, 82, 83, 84, 85, 86, 87,
        104, 105, 158, 107, 21, 109, 110, 111, 96, 97, 2, 12, 100, 30, 102, 103,
        120, 155, 122, 123, 124, 125, 126, 127, 112, 113, 114, 115, 116, 117, 118, 119,
        136, 137, 138, 139, 5, 141, 142, 143, 128, 129, 130, 131, 132, 133, 230, 135,
        152, 153, 154, 77, 156, 157, 78, 159, 144, 145, 146, 147, 101, 149, 150, 151,
        168, 169, 170, 171, 172, 173, 174, 175, 160, 161, 162, 225, 164, 165, 166, 167,
        184, 185, 186, 187, 188, 189, 190, 191, 211, 177, 178, 179, 180, 181, 106, 183,
        200, 201, 202, 203, 204, 205, 206, 207, 25, 193, 194, 195, 196, 197, 198, 199,
        224, 217, 218, 219, 220, 221, 222, 231, 208, 209, 210, 192, 212, 228, 214, 215,
        232, 241, 234, 235, 236, 237, 246, 239, 216, 35, 226, 227, 148, 229, 134, 223,
        248, 249, 81, 251, 252, 67, 254, 255, 240, 233, 99, 243, 244, 245, 238, 247,
    ),
    (
        8, 9, 18, 11, 12, 21, 14, 15, 0, 1, 2, 149, 188, 5, 6, 7,
        24, 33, 26, 27, 28, 29, 38, 31, 16, 17, 10, 19, 20, 13, 22, 23,
        48, 41, 42, 43, 44, 45, 46, 55, 32, 25, 34, 35, 36, 37, 30, 39,
        56, 57, 58, 59, 60, 61, 62, 63, 40, 49, 50, 51, 52, 53, 54, 47,
        72, 73, 74, 75, 251, 77, 78, 79, 64, 65, 66, 67, 68, 69, 70, 71,
        88, 89, 90, 91, 92, 93, 94, 95, 80, 81, 82, 83, 84, 85, 86, 87,
        104, 105, 106, 107, 108, 109, 110, 111, 96, 97, 98, 99, 100, 101, 102, 103,
        120, 121, 122, 123, 124, 125, 126, 127, 112, 113, 114, 115, 116, 117, 118, 119,
        136, 137, 138, 139, 140, 141, 142, 143, 128, 129, 130, 131, 132, 133, 134, 135,
        152, 153, 154, 155, 156, 157, 158, 159, 3, 145, 146, 147, 148, 144, 150, 151,
        168, 169, 170, 171, 172, 173, 174, 175, 160, 161, 162, 163, 164, 165, 166, 167,
        184, 185, 186, 187, 4, 189, 190, 191, 176, 177, 178, 179, 180, 181, 182, 183,
        208, 201, 202, 203, 204, 205, 206, 215, 192, 193, 194, 195, 196, 197, 198, 199,
        216, 225, 218, 219, 220, 221, 230, 223, 200, 209, 210, 211, 212, 213, 214, 207,
        232, 233, 242, 235, 236, 245, 238, 239, 224, 217, 226, 227, 228, 229, 222, 231,
        248, 249, 250, 76, 255, 253, 254, 252, 240, 241, 234, 243, 244, 237, 246, 247,
    ),
    (
        8, 9, 10, 19, 20, 13, 14, 15, 0, 1, 2, 3, 239, 5, 6, 7,
        24, 25, 34, 27, 28, 37, 30, 31, 16, 17, 18, 11, 12, 21, 22, 23,
        40, 49, 42, 43, 44, 45, 54, 47, 32, 33, 26, 35, 36, 29, 38, 39,
        64, 57, 58, 59, 60, 61, 62, 71, 48, 41, 50, 51, 52, 53, 46, 55,
        72, 73, 74, 75, 76, 77, 78, 79, 56, 65, 66, 67, 68, 69, 70, 63,
        88, 89, 90, 91, 92, 93, 94, 95, 80, 81, 82, 83, 84, 85, 86, 87,
        104, 105, 106, 107, 108, 109, 110, 111, 96, 97, 98, 99, 100, 101, 102, 103,
        120, 121, 122, 123, 124, 125, 126, 127, 112, 113, 114, 115, 116, 117, 118, 119,
        136, 137, 138, 139, 140, 141, 142, 143, 128, 129, 130, 131, 132, 133, 134, 135,
        152, 153, 154, 155, 156, 157, 158, 159, 144, 145, 146, 147, 148, 149, 150, 151,
        168, 169, 170, 171, 172, 173, 174, 175, 160, 161, 162, 163, 164, 165, 166, 167,
        192, 185, 186, 187, 188, 189, 190, 199, 176, 177, 178, 179, 180, 181, 182, 183,
        200, 209, 202, 203, 204, 205, 214, 207, 184, 193, 194, 195, 196, 197, 198, 191,
        216, 217, 226, 219, 220, 229, 222, 223, 208, 201, 210, 211, 212, 213, 206, 215,
        232, 233, 234, 243, 244, 237, 238, 4, 224, 225, 218, 227, 228, 221, 230, 231,
        248, 249, 250, 251, 252, 253, 254, 255, 240, 241, 242, 235, 236, 245, 246, 247,
    ),
    (
        8, 9, 10, 19, 20, 13, 14, 15, 0, 1, 2, 3, 46, 5, 6, 7,
        24, 25, 26, 35, 36, 29, 30, 31, 16, 17, 18, 11, 12, 21, 22, 23,
        40, 41, 50, 43, 44, 53, 255, 47, 32, 33, 34, 27, 28, 37, 38, 39,
        56, 65, 58, 59, 60, 61, 70, 63, 48, 49, 42, 51, 52, 45, 54, 55,
        80, 73, 74, 75, 76, 77, 121, 87, 64, 57, 66, 67, 68, 69, 62, 71,
        88, 89, 90, 91, 92, 93, 94, 95, 72, 81, 82, 83, 84, 85, 86, 79,
        104, 105, 106, 107, 108, 109, 110, 111, 96, 97, 98, 99, 100, 101, 102, 103,
        120, 78, 122, 123, 124, 125, 126, 127, 112, 113, 114, 115, 116, 117, 118, 119,
        136, 137, 138, 139, 140, 141, 142, 143, 128, 129, 130, 131, 132, 133, 134, 135,
        152, 153, 154, 155, 156, 157, 158, 159, 144, 145, 146, 147, 148, 149, 150, 151,
        176, 169, 170, 171, 172, 173, 174, 183, 160, 161, 162, 163, 164, 165, 166, 167,
        184, 193, 186, 187, 188, 189, 198, 191, 168, 177, 178, 179, 180, 181, 182, 175,
        200, 201, 210, 203, 204, 213, 206, 207, 192, 185, 194, 195, 196, 197, 190, 199,
        216, 217, 218, 227, 228, 221, 222, 223, 208, 209, 202, 211, 212, 205, 214, 215,
        232, 233, 234, 243, 244, 237, 238, 239, 224, 225, 226, 219, 220, 229, 230, 231,
        248, 249, 250, 251, 252, 253, 254, 4, 240, 241, 242, 235, 236, 245, 246, 247,
    ),
    (
        8, 9, 18, 11, 12, 21, 14, 15, 0, 1, 2, 3, 4, 5, 6, 7,
        24, 25, 26, 35, 36, 29, 30, 31, 16, 17, 10, 19, 20, 13, 22, 23,
        40, 41, 42, 51, 52, 45, 46, 47, 32, 33, 34, 27, 28, 37, 38, 39,
        56, 57, 66, 59, 60, 69, 62, 63, 48, 49, 50, 43, 44, 53, 54, 55,
        72, 81, 74, 75, 76, 77, 86, 79, 64, 65, 58, 67, 68, 61, 70, 71,
        96, 89, 90, 91, 92, 93, 94, 103, 80, 73, 82, 83, 84, 85, 78, 87,
        104, 105, 106, 107, 108, 109, 110, 111, 88, 97, 98, 99, 100, 101, 102, 95,
        120, 121, 122, 123, 124, 125, 126, 127, 112, 113, 114, 115, 116, 117, 118, 119,
        136, 137, 138, 139, 140, 141, 142, 143, 128, 129, 130, 131, 132, 133, 134, 135,
        160, 153, 154, 155, 156, 157, 158, 167, 144, 145, 146, 147, 148, 149, 150, 151,
        168, 177, 170, 171, 172, 173, 182, 175, 152, 161, 162, 163, 164, 165, 166, 159,
        184, 185, 194, 187, 188, 197, 190, 191, 176, 169, 178, 179, 180, 181, 174, 183,
        200, 201, 202, 211, 212, 205, 206, 207, 192, 193, 186, 195, 196, 189, 198, 199,
        216, 217, 218, 227, 228, 221, 222, 223, 208, 209, 210, 203, 204, 213, 214, 215,
        232, 233, 242, 235, 236, 245, 238, 239, 224, 225, 226, 219, 220, 229, 230, 231,
        248, 249, 250, 251, 252, 253, 254, 255, 240, 241, 234, 243, 244, 237, 246, 247,
    ),
    (
        8, 17, 10, 11, 12, 13, 22, 15, 0, 1, 2, 3, 4, 5, 6, 7,
        24, 25, 34, 27, 28, 37, 30, 31, 16, 9, 18, 19, 20, 21, 14, 23,
        40, 41, 83, 51, 52, 201, 46, 47, 32, 33, 26, 35, 36, 29, 38, 39,
        56, 57, 58, 67, 68, 61, 62, 63, 48, 49, 50, 43, 44, 53, 54, 55,
        72, 73, 82, 75, 76, 85, 78, 79, 64, 65, 66, 59, 60, 69, 70, 71,
        88, 97, 90, 91, 92, 93, 102, 95, 80, 81, 74, 42, 84, 77, 86, 87,
        112, 105, 106, 107, 108, 109, 110, 119, 96, 89, 98, 213, 100, 101, 94, 103,
        120, 121, 122, 123, 124, 125, 126, 127, 104, 113, 114, 115, 116, 117, 118, 111,
        144, 137, 138, 139, 140, 141, 142, 151, 128, 129, 130, 131, 132, 133, 134, 135,
        152, 161, 154, 155, 156, 157, 166, 159, 136, 145, 146, 147, 148, 149, 150, 143,
        168, 169, 178, 171, 172, 181, 174, 175, 160, 153, 162, 163, 164, 165, 158, 167,
        184, 185, 186, 195, 196, 189, 190, 191, 176, 177, 170, 179, 180, 173, 182, 183,
        200, 45, 202, 211, 212, 205, 206, 207, 192, 193, 194, 187, 188, 197, 198, 199,
        216, 217, 226, 219, 220, 229, 99, 223, 208, 209, 215, 203, 204, 222, 214, 210,
        232, 241, 234, 235, 236, 237, 246, 239, 224, 225, 218, 227, 228, 221, 230, 231,
        248, 249, 250, 251, 252, 253, 254, 255, 240, 233, 242, 243, 244, 245, 238, 247,
    ),
    None,
    None,
    None,
    None,
    None,
    None,
    None,
    None,
)
COL_FILL = (
    (
        1, 9, 10, 11, 12, 13, 14, 6, 0, 8, 2, 3, 4, 5, 15, 7,
        24, 25, 26, 27, 28, 29, 30, 31, 16, 17, 18, 19, 20, 21, 22, 23,
        40, 41, 42, 43, 44, 45, 46, 47, 32, 33, 34, 35, 36, 37, 38, 39,
        56, 57, 58, 59, 60, 61, 62, 63, 48, 49, 50, 51, 52, 53, 54, 55,
        72, 73, 74, 75, 76, 77, 78, 79, 64, 65, 66, 67, 68, 69, 70, 71,
        88, 89, 90, 91, 92, 93, 94, 95, 80, 81, 82, 83, 84, 85, 86, 87,
        104, 105, 106, 107, 108, 109, 110, 111, 96, 97, 98, 99, 100, 101, 102, 103,
        120, 121, 122, 123, 124, 125, 126, 127, 112, 113, 114, 115, 116, 117, 118, 119,
        136, 137, 138, 139, 140, 141, 142, 143, 128, 129, 130, 131, 132, 133, 134, 135,
        152, 153, 154, 155, 156, 157, 158, 159, 144, 145, 146, 147, 148, 149, 150, 151,
        168, 169, 170, 171, 172, 173, 174, 175, 160, 161, 162, 163, 164, 165, 166, 167,
        184, 185, 186, 187, 188, 189, 190, 191, 176, 177, 178, 179, 180, 181, 182, 183,
        200, 201, 202, 203, 204, 205, 206, 207, 192, 193, 194, 195, 196, 197, 198, 199,
        216, 217, 218, 219, 220, 221, 222, 223, 208, 209, 210, 211, 212, 213, 214, 215,
        232, 233, 234, 235, 236, 237, 238, 239, 224, 225, 226, 227, 228, 229, 230, 231,
        248, 240, 250, 251, 252, 253, 247, 255, 249, 241, 242, 243, 244, 245, 246, 254,
    ),
    (
        8, 2, 10, 11, 12, 13, 5, 15, 0, 1, 9, 3, 4, 14, 6, 7,
        17, 25, 26, 27, 28, 29, 30, 22, 16, 24, 18, 19, 20, 21, 31, 23,
        40, 41, 42, 43, 44, 45, 46, 47, 32, 33, 34, 35, 36, 37, 38, 39,
        56, 57, 58, 59, 60, 61, 62, 63, 48, 49, 50, 51, 52, 53, 54, 55,
        72, 73, 74, 75, 76, 77, 78, 79, 64, 65, 66, 67, 68, 69, 70, 71,
        88, 89, 90, 91, 92, 93, 94, 95, 80, 81, 82, 83, 84, 85, 86, 87,
        104, 105, 106, 107, 108, 109, 110, 111, 96, 97, 98, 99, 100, 101, 102, 103,
        120, 121, 122, 123, 124, 125, 126, 127, 112, 113, 114, 115, 116, 117, 118, 119,
        136, 137, 138, 139, 140, 141, 142, 143, 128, 129, 130, 131, 132, 133, 134, 135,
        152, 153, 154, 155, 156, 157, 158, 159, 144, 145, 146, 147, 148, 149, 150, 151,
        168, 169, 170, 171, 172, 173, 174, 175, 160, 161, 162, 163, 164, 165, 166, 167,
        184, 185, 186, 187, 188, 189, 190, 191, 176, 177, 178, 179, 180, 181, 182, 183,
        200, 201, 202, 203, 204, 205, 206, 207, 192, 193, 194, 195, 196, 197, 198, 199,
        216, 217, 218, 219, 220, 221, 222, 223, 208, 209, 210, 211, 212, 213, 214, 215,
        232, 224, 234, 235, 236, 237, 231, 239, 233, 225, 226, 227, 228, 229, 230, 238,
        248, 249, 241, 251, 252, 246, 254, 255, 240, 250, 242, 243, 244, 245, 253, 247,
    ),
    (
        8, 9, 3, 11, 12, 4, 14, 15, 0, 1, 2, 10, 13, 5, 6, 7,
        24, 18, 26, 27, 28, 29, 21, 31, 16, 17, 25, 19, 20, 30, 22, 23,
        33, 41, 42, 43, 44, 45, 46, 38, 32, 40, 34, 35, 36, 37, 47, 39,
        56, 57, 58, 59, 60, 61, 62, 63, 48, 49, 50, 51, 52, 53, 54, 55,
        72, 73, 74, 75, 76, 77, 78, 79, 64, 65, 66, 67, 68, 69, 70, 71,
        88, 89, 90, 91, 92, 93, 94, 95, 80, 81, 82, 83, 84, 85, 86, 87,
        104, 105, 106, 107, 108, 109, 110, 111, 96, 97, 98, 99, 100, 101, 102, 103,
        120, 121, 122, 123, 124, 125, 126, 127, 112, 113, 114, 115, 116, 117, 118, 119,
        136, 137, 138, 139, 140, 141, 142, 143, 128, 129, 130, 131, 132, 133, 134, 135,
        152, 153, 154, 155, 156, 157, 158, 159, 144, 145, 146, 147, 148, 149, 150, 151,
        168, 169, 170, 171, 172, 173, 174, 175, 160, 161, 162, 163, 164, 165, 166, 167,
        184, 185, 186, 187, 188, 189, 190, 191, 176, 177, 178, 179, 180, 181, 182, 183,
        200, 201, 202, 203, 204, 205, 206, 207, 192, 193, 194, 195, 196, 197, 198, 199,
        216, 208, 218, 219, 220, 221, 215, 223, 217, 209, 210, 211, 212, 213, 214, 222,
        232, 233, 225, 235, 236, 230, 238, 239, 224, 234, 226, 227, 228, 229, 237, 231,
        248, 249, 250, 242, 245, 253, 254, 255, 240, 241, 251, 243, 244, 252, 246, 247,
    ),
    (
        8, 9, 10, 4, 3, 13, 14, 15, 0, 1, 2, 12, 11, 5, 6, 7,
        24, 25, 19, 27, 28, 20, 30, 31, 16, 17, 18, 26, 29, 21, 22, 23,
        40, 34, 42, 43, 44, 45, 37, 47, 32, 33, 41, 35, 36, 46, 38, 39,
        49, 57, 58, 59, 60, 61, 62, 54, 48, 56, 50, 51, 52, 53, 63, 55,
        72, 73, 74, 75, 76, 77, 78, 79, 64, 65, 66, 67, 68, 69, 70, 71,
        88, 89, 90, 91, 92, 93, 94, 95, 80, 81, 82, 83, 84, 85, 86, 87,
        104, 105, 106, 107, 108, 109, 110, 111, 96, 97, 98, 99, 100, 101, 102, 103,
        120, 121, 122, 123, 124, 125, 126, 127, 112, 113, 114, 115, 116, 117, 118, 119,
        136, 137, 138, 139, 140, 141, 142, 143, 128, 129, 130, 131, 132, 133, 134, 135,
        152, 153, 154, 155, 156, 157, 158, 159, 144, 145, 146, 147, 148, 149, 150, 151,
        168, 169, 170, 171, 172, 173, 174, 175, 160, 161, 162, 163, 164, 165, 166, 167,
        184, 185, 186, 187, 188, 189, 190, 191, 176, 177, 178, 179, 180, 181, 182, 183,
        200, 192, 202, 203, 204, 205, 199, 207, 201, 193, 194, 195, 196, 197, 198, 206,
        216, 217, 209, 219, 220, 214, 222, 223, 208, 218, 210, 211, 212, 213, 221, 215,
        232, 233, 234, 226, 229, 237, 238, 239, 224, 225, 235, 227, 228, 236, 230, 231,
        248, 249, 250, 244, 243, 253, 254, 255, 240, 241, 242, 252, 251, 245, 246, 247,
    ),
    (
        8, 9, 10, 2, 5, 13, 14, 15, 0, 1, 11, 3, 4, 12, 6, 7,
        24, 25, 26, 20, 19, 29, 30, 31, 16, 17, 18, 28, 27, 21, 22, 23,
        40, 41, 35, 43, 44, 36, 46, 47, 32, 33, 34, 42, 45, 37, 38, 39,
        56, 50, 58, 59, 60, 61, 53, 63, 48, 49, 57, 51, 52, 62, 54, 55,
        65, 73, 74, 75, 76, 77, 78, 70, 64, 72, 66, 67, 68, 69, 79, 71,
        88, 89, 90, 91, 92, 93, 94, 95, 80, 81, 82, 83, 84, 85, 86, 87,
        104, 105, 106, 107, 108, 109, 110, 111, 96, 97, 98, 99, 100, 101, 102, 103,
        120, 121, 122, 123, 124, 125, 126, 127, 112, 113, 114, 115, 116, 117, 118, 119,
        136, 137, 138, 139, 140, 141, 142, 143, 128, 129, 130, 131, 132, 133, 134, 135,
        152, 153, 154, 155, 156, 157, 158, 159, 144, 145, 146, 147, 148, 149, 150, 151,
        168, 169, 170, 171, 172, 173, 174, 175, 160, 161, 162, 163, 164, 165, 166, 167,
        184, 176, 186, 187, 188, 189, 183, 191, 185, 177, 178, 179, 180, 181, 182, 190,
        200, 201, 193, 203, 204, 198, 206, 207, 192, 202, 194, 195, 196, 197, 205, 199,
        216, 217, 218, 210, 213, 221, 222, 223, 208, 209, 219, 211, 212, 220, 214, 215,
        232, 233, 234, 228, 227, 237, 238, 239, 224, 225, 226, 236, 235, 229, 230, 231,
        248, 249, 243, 251, 252, 244, 254, 255, 240, 241, 242, 250, 253, 245, 246, 247,
    ),
    (
        8, 9, 1, 11, 12, 6, 14, 15, 0, 10, 2, 3, 4, 5, 13, 7,
        24, 25, 26, 18, 21, 29, 30, 31, 16, 17, 27, 19, 20, 28, 22, 23,
        40, 41, 42, 36, 35, 45, 46, 47, 32, 33, 34, 44, 43, 37, 38, 39,
        56, 57, 51, 59, 60, 52, 62, 63, 48, 49, 50, 58, 61, 53, 54, 55,
        72, 66, 74, 75, 76, 77, 69, 79, 64, 65, 73, 67, 68, 78, 70, 71,
        81, 89, 90, 91, 92, 93, 94, 86, 80, 88, 82, 83, 84, 85, 95, 87,
        104, 105, 106, 107, 108, 109, 110, 111, 96, 97, 98, 99, 100, 101, 102, 103,
        120, 121, 122, 123, 124, 125, 126, 127, 112, 113, 114, 115, 116, 117, 118, 119,
        136, 137, 138, 139, 140, 141, 142, 143, 128, 129, 130, 131, 132, 133, 134, 135,
        152, 153, 154, 155, 156, 157, 158, 159, 144, 145, 146, 147, 148, 149, 150, 151,
        168, 160, 170, 171, 172, 173, 167, 175, 169, 161, 162, 163, 164, 165, 166, 174,
        184, 185, 177, 187, 188, 182, 190, 191, 176, 186, 178, 179, 180, 181, 189, 183,
        200, 201, 202, 194, 197, 205, 206, 207, 192, 193, 203, 195, 196, 204, 198, 199,
        216, 217, 218, 212, 211, 221, 222, 223, 208, 209, 210, 220, 219, 213, 214, 215,
        232, 233, 227, 235, 236, 228, 238, 239, 224, 225, 226, 234, 237, 229, 230, 231,
        248, 242, 250, 251, 252, 253, 245, 255, 240, 241, 249, 243, 244, 254, 246, 247,
    ),
    (
        8, 0, 10, 11, 36, 13, 7, 15, 9, 1, 2, 12, 4, 5, 6, 14,
        24, 25, 17, 27, 28, 22, 30, 31, 16, 26, 18, 19, 20, 21, 29, 23,
        40, 41, 3, 34, 37, 79, 46, 47, 32, 210, 43, 35, 42, 44, 38, 39,
        56, 57, 58, 52, 51, 61, 62, 63, 48, 49, 50, 60, 59, 53, 54, 55,
        72, 73, 67, 75, 76, 68, 78, 45, 64, 65, 66, 74, 77, 69, 70, 71,
        88, 82, 90, 91, 92, 93, 85, 95, 80, 81, 89, 83, 84, 94, 86, 87,
        97, 105, 106, 107, 108, 109, 110, 102, 96, 104, 98, 99, 100, 101, 111, 103,
        120, 121, 122, 123, 124, 125, 126, 127, 112, 113, 114, 115, 116, 117, 118, 119,
        136, 137, 138, 139, 140, 141, 142, 143, 128, 129, 130, 131, 132, 133, 134, 135,
        152, 144, 154, 155, 156, 157, 151, 159, 153, 145, 146, 147, 148, 149, 150, 158,
        168, 169, 161, 171, 172, 166, 174, 175, 160, 170, 162, 163, 164, 165, 173, 167,
        184, 185, 186, 178, 181, 189, 190, 191, 249, 177, 187, 179, 180, 188, 182, 183,
        200, 201, 202, 196, 195, 205, 206, 207, 192, 193, 194, 204, 203, 197, 198, 199,
        216, 217, 211, 219, 220, 212, 222, 223, 208, 209, 33, 218, 221, 176, 214, 215,
        232, 226, 234, 235, 236, 237, 229, 239, 224, 225, 233, 227, 228, 238, 230, 231,
        241, 213, 250, 251, 252, 253, 254, 246, 240, 248, 242, 243, 244, 245, 255, 247,
    ),
    None,
    None,
    None,
    None,
    None,
    None,
    None,
    None,
)


def tick_pairs(n_row, n_col):
    chips = n_row // 2
    ticks = chips + n_col - 1
    rows = [[] for _ in range(ticks)]
    cols = [[] for _ in range(ticks)]
    for chip in range(chips):
        for core in range(2):
            for col in range(n_col):
                for step in (1, -1):
                    place = chip if core == 0 else chips - 1 - chip
                    place += col if step > 0 else n_col - 1 - col
                    here = (2 * chip + core) * n_col + col
                    onward = chip + 1 - 2 * core
                    if 0 <= onward < chips:
                        rows[place].append((here, (2 * onward + core) * n_col + col))
                    if 0 <= col + step < n_col:
                        cols[place].append((here, (2 * chip + core) * n_col + col + step))
    return rows[:-1], cols[:-1]


def patterns(pairs, fills):
    result = [None] * len(pairs)
    for group, fill in zip(GROUPS, fills):
        together = sorted({pair for t in group for pair in pairs[t]})
        if fill is not None:
            assert all(fill[a] == b for a, b in together)
            together = list(enumerate(fill))
        for t in group:
            result[t] = tuple(together)
    return result


def swaps(n_row, n_col):
    chip, off, even, odd = [], [], [], []
    for row in range(n_row):
        for col in range(n_col):
            here = row * n_col + col
            chip.append((here, (row ^ 1) * n_col + col))
            other = row + 1 if row % 2 else row - 1
            if 0 <= other < n_row:
                off.append((here, other * n_col + col))
            else:
                off.append((here, row * n_col + (col ^ 1)))
            even.append((here, row * n_col + (col ^ 1)))
            side = col + 1 if col % 2 else col - 1
            if 0 <= side < n_col:
                odd.append((here, row * n_col + side))
            else:
                odd.append((here, (row ^ 1) * n_col + col))
    return chip, off, even, odd


def whole(count):
    return [pl.BlockSpec(memory_space=pltpu.VMEM)] * count


def call(kernel, inputs, outputs, cost, specs=None, scratch=(), aliases=None, limit=16 << 20):
    return pl.pallas_call(
        kernel,
        out_shape=outputs,
        in_specs=specs or whole(len(inputs)),
        out_specs=jax.tree.map(lambda _: pl.BlockSpec(memory_space=pltpu.VMEM), outputs),
        scratch_shapes=list(scratch),
        input_output_aliases=aliases or {},
        cost_estimate=pl.CostEstimate(flops=cost, bytes_accessed=1 << 16, transcendentals=0),
        compiler_params=pltpu.CompilerParams(vmem_limit_bytes=limit),
    )(*inputs)


def dot(a, b):
    return jnp.dot(a, b, preferred_element_type=F32)


def span(index, width):
    if isinstance(index, int):
        return pl.ds(index * width, width)
    return pl.ds(pl.multiple_of(index * width, width), width)


def gather_kernel(side, op_ref, out_ref, sems):
    core = lax.rem(lax.axis_index("row"), 2)
    into, out = 1 - core, core
    blocks = [(into, out)]
    blocks += [(into, 3 - h) for h in range(2)]
    blocks += [(2 + h, out) for h in range(2)]
    blocks += [(2 + h, 3 - h) for h in range(2)]
    copies = []
    for n, (a, b) in enumerate(blocks):
        copies.append(
            pltpu.make_async_copy(
                op_ref.at[0, 0, span(a, side), span(b, side)], out_ref.at[n], sems.at[n]
            )
        )
    for copy in copies:
        copy.start()
    for copy in copies:
        copy.wait()


def base_kernel(chunk, forcing_ref, op_ref, held_ref, base_ref, send_ref, half_ref, sems):
    order = held_ref.shape[0]
    side = order // 4
    steps = order // chunk
    core = lax.rem(lax.axis_index("row"), 2)

    def copy(n):
        return pltpu.make_async_copy(
            op_ref.at[0, 0, span(n, chunk), :], held_ref.at[span(n, chunk), :], sems.at[n]
        )

    for n in range(steps):
        copy(n).start()
    half_ref[...] = forcing_ref[0, 0].astype(BF16)
    base_ref[...] = jnp.zeros_like(base_ref)

    def step(n, carry):
        copy(n).wait()
        base_ref[...] += dot(half_ref[:, span(n, chunk)], held_ref[span(n, chunk), :])
        return carry

    lax.fori_loop(0, steps, step, 0)
    send_ref[:, :side] = base_ref[:, span(core, side)]
    send_ref[:, side:] = base_ref[:, 2 * side :]


def place(t, n_row, n_col):
    row, col = lax.axis_index("row"), lax.axis_index("col")
    core, chip = lax.rem(row, 2), lax.div(row, 2)
    last = n_row // 2 - 1
    down = jnp.where(core == 0, chip, last - chip)
    first = down + col == t
    second = down + n_col - 1 - col == t
    head = jnp.where(second, 1, 0)
    row_edge = down == 0
    col_edge = jnp.where(second, col == n_col - 1, col == 0)
    return core, head, jnp.logical_or(first, second), row_edge, col_edge


def unless(edge, value):
    return jnp.where(edge, jnp.zeros_like(value), value)


def row_kernel(t, n_row, n_col, row_ref, col_ref, held_ref, near_ref, base_ref, far_ref, mid_ref, out_ref):
    core, head, active, row_edge, col_edge = place(t, n_row, n_col)
    loads, side = row_ref.shape

    @pl.when(active)
    def _():
        out = 1 - core
        row_in = unless(row_edge, row_ref[...])
        own = unless(col_edge, col_ref[:loads])
        value = base_ref[:, span(out, side)]
        value += dot(row_in, held_ref[span(core, side), span(out, side)])
        value += dot(own, held_ref[span(2 + head, side), span(out, side)])
        mid_ref[...] = value.astype(BF16)
        other = unless(col_edge, col_ref[loads:])
        value = far_ref[:, :side]
        value += dot(other, near_ref[3 + head])
        value += dot(mid_ref[...], near_ref[0])
        out_ref[...] = value.astype(BF16)


def col_kernel(
    t, n_row, n_col, row_ref, col_ref, mid_ref, held_ref, near_ref, base_ref, far_base_ref, *refs
):
    out_ref, own_ref, far_ref = refs[-3:]
    core, head, active, row_edge, col_edge = place(t, n_row, n_col)
    loads, side = row_ref.shape

    @pl.when(active)
    def _():
        out = 3 - head
        row_in = unless(row_edge, row_ref[...])
        own = unless(col_edge, col_ref[:loads])
        value = base_ref[:, span(out, side)]
        value += dot(row_in, held_ref[span(core, side), span(out, side)])
        value += dot(own, held_ref[span(2 + head, side), span(out, side)])
        out_ref[:loads] = value.astype(BF16)
        other = unless(col_edge, col_ref[loads:])
        value = far_base_ref[:, span(2 - head, side)]
        value += dot(mid_ref[...], near_ref[1 + head])
        value += dot(other, near_ref[5 + head])
        out_ref[loads:] = value.astype(BF16)
        own_ref[2 * head] = row_in
        own_ref[2 * head + 1] = own
        far_ref[2 * head] = mid_ref[...]
        far_ref[2 * head + 1] = other


def last_kernel(t, n_row, n_col, row_ref, col_ref, held_ref, base_ref, old_own, old_far, own_ref, far_ref):
    core, head, active, row_edge, col_edge = place(t, n_row, n_col)
    loads, side = row_ref.shape

    @pl.when(active)
    def _():
        out = 1 - core
        row_in = unless(row_edge, row_ref[...])
        own = unless(col_edge, col_ref[:loads])
        other = unless(col_edge, col_ref[loads:])
        value = base_ref[:, span(out, side)]
        value += dot(row_in, held_ref[span(core, side), span(out, side)])
        value += dot(own, held_ref[span(2 + head, side), span(out, side)])
        own_ref[2 * head] = row_in
        own_ref[2 * head + 1] = own
        far_ref[2 * head] = value.astype(BF16)
        far_ref[2 * head + 1] = other


def sum_kernel(own_ref, other_ref, held_ref, base_ref, out_ref, chip_ref, off_ref, even_ref, odd_ref, left_ref):
    core = lax.rem(lax.axis_index("row"), 2)
    parity = lax.rem(lax.axis_index("col"), 2)
    side = own_ref.shape[-1]

    def wide(ref, n):
        return ref[n].astype(F32)

    left_ref[:, span(core, side)] = ((wide(own_ref, 0) + wide(own_ref, 2)) * 0.25).astype(BF16)
    left_ref[:, span(1 - core, side)] = (
        (wide(other_ref, 0) + wide(other_ref, 2)) * 0.25
    ).astype(BF16)
    for h in range(2):
        both = wide(own_ref, 2 * h + 1) + wide(other_ref, 2 * h + 1)
        left_ref[:, span(2 + h, side)] = (both * 0.25).astype(BF16)
    for n in range(4):
        out_ref[:, span(n, side)] = base_ref[:, span(n, side)] + dot(
            left_ref[...], held_ref[:, span(n, side)]
        )
    chip_ref[...] = out_ref[:, span(1 - core, side)].astype(BF16)
    off_ref[...] = out_ref[:, span(core, side)].astype(BF16)
    even_ref[...] = out_ref[:, span(3 - parity, side)].astype(BF16)
    odd_ref[...] = out_ref[:, span(2 + parity, side)].astype(BF16)


def residual_kernel(n_row, n_col, forcing_ref, pre_ref, coupling_ref, chip_ref, off_ref, even_ref, odd_ref, pre_out, out_ref):
    row, col = lax.axis_index("row"), lax.axis_index("col")
    core, parity = lax.rem(row, 2), lax.rem(col, 2)
    side = chip_ref.shape[-1]

    def finish(index, facing):
        block = span(index, side)
        pre = pre_ref[:, block]
        pre_out[0, 0, :, block] = pre
        out_ref[0, 0, :, block] = (
            forcing_ref[0, 0, :, block] - pre + coupling_ref[:, block] * (facing - pre)
        )

    row_end = jnp.logical_or(row == 0, row == n_row - 1)
    col_end = jnp.logical_or(col == 0, col == n_col - 1)
    finish(1 - core, chip_ref[...].astype(F32))
    finish(core, unless(row_end, off_ref[...].astype(F32)))
    finish(3 - parity, even_ref[...].astype(F32))
    finish(2 + parity, unless(col_end, odd_ref[...].astype(F32)))


def local(n_row, n_col, forcing, local_op, material, stiffness):
    loads, order = forcing.shape[2:]
    side = order // 4
    chunk = side
    chip_swap, off_swap, even_swap, odd_swap = swaps(n_row, n_col)
    row_pairs, col_pairs = tick_pairs(n_row, n_col)
    row_sets = patterns(row_pairs, ROW_FILL)
    col_sets = patterns(col_pairs, COL_FILL)

    def vmem(shape, dtype):
        return pltpu.VMEM(shape, dtype)

    def shift(value, pairs):
        return lax.ppermute(value, AXES, pairs)

    anywhere = pl.BlockSpec(memory_space=pltpu.HBM)
    local_op = pltpu.with_memory_space_constraint(local_op, pltpu.HBM)
    parcel = call(
        functools.partial(gather_kernel, side),
        (local_op,),
        vmem((7, side, side), BF16),
        1 << 20,
        specs=[anywhere],
        scratch=[pltpu.SemaphoreType.DMA((7,))],
    )
    near = shift(parcel, chip_swap)
    held, base, base_parcel = call(
        functools.partial(base_kernel, chunk),
        (forcing, local_op),
        (
            vmem((order, order), BF16),
            vmem((loads, order), F32),
            vmem((loads, 3 * side), F32),
        ),
        2 * loads * order * order,
        specs=[pl.BlockSpec(memory_space=pltpu.VMEM), anywhere],
        scratch=[pltpu.VMEM((loads, order), BF16), pltpu.SemaphoreType.DMA((order // chunk,))],
    )
    far = shift(base_parcel, chip_swap)
    classes = jnp.arange(stiffness.shape[0], dtype=jnp.int32)
    coupling = jnp.sum(
        jnp.where(material[0, 0][None, :] == classes[:, None], stiffness[:, None], 0.0), axis=0
    )[None, :]

    row_in = jnp.zeros((loads, side), BF16)
    col_in = jnp.zeros((2 * loads, side), BF16)
    kept = ()
    steps = len(row_sets)
    work = 8 * loads * side * side
    traces = (vmem((4, loads, side), BF16),) * 2
    for t in range(steps):
        mid, row_out = call(
            functools.partial(row_kernel, t, n_row, n_col),
            (row_in, col_in, held, near, base, far),
            (vmem((loads, side), BF16), vmem((loads, side), BF16)),
            work,
        )
        row_next = shift(row_out, row_sets[t])
        col_out, *kept = call(
            functools.partial(col_kernel, t, n_row, n_col),
            (row_in, col_in, mid, held, near, base, far, *kept),
            (vmem((2 * loads, side), BF16), *traces),
            work,
            aliases={7: 1, 8: 2} if kept else None,
        )
        col_next = shift(col_out, col_sets[t])
        row_in, col_in = row_next, col_next
    own, away = call(
        functools.partial(last_kernel, steps, n_row, n_col),
        (row_in, col_in, held, base, *kept),
        traces,
        work,
        aliases={4: 0, 5: 1},
    )
    other = shift(away, chip_swap)
    trace = vmem((loads, side), BF16)
    pre, chip, off, even, odd = call(
        sum_kernel,
        (own, other, held, base),
        (vmem((loads, order), F32), trace, trace, trace, trace),
        2 * loads * order * order,
        scratch=[pltpu.VMEM((loads, order), BF16)],
    )
    arrived = (
        shift(chip, chip_swap),
        shift(off, off_swap),
        shift(even, even_swap),
        shift(odd, odd_swap),
    )
    shape = jax.ShapeDtypeStruct((1, 1, loads, order), F32)
    return tuple(
        call(
            functools.partial(residual_kernel, n_row, n_col),
            (forcing, pre, coupling, *arrived),
            (shape, shape),
            1 << 20,
        )
    )


def solution(mesh):
    n_row, n_col = mesh.shape["row"], mesh.shape["col"]
    return jax.shard_map(
        functools.partial(local, n_row, n_col),
        mesh=mesh,
        in_specs=(
            P("row", "col", None, None),
            P("row", "col", None, None),
            P("row", "col", None),
            P(),
        ),
        out_specs=(P("row", "col", None, None), P("row", "col", None, None)),
        check_vma=False,
    )
```

```python
import functools

import jax
import jax.numpy as jnp
from jax import lax
from jax.experimental import pallas as pl
from jax.experimental.pallas import tpu as pltpu
from jax.sharding import PartitionSpec as P


BF16 = jnp.bfloat16
F32 = jnp.float32
AXES = ("row", "col")
GROUPS = (
    (0, 21,),
    (1, 20,),
    (2, 19,),
    (3, 18,),
    (4, 17,),
    (5, 16,),
    (6, 15,),
    (7,),
    (8,),
    (9,),
    (10,),
    (11,),
    (12,),
    (13,),
    (14,),
)
ROW_FILL = (
    (
        16, 9, 1, 11, 12, 13, 14, 23, 192, 201, 2, 3, 4, 5, 6, 7,
        24, 25, 10, 26, 28, 29, 30, 31, 8, 17, 18, 19, 20, 21, 22, 15,
        40, 41, 42, 43, 44, 45, 46, 47, 32, 33, 34, 35, 36, 37, 38, 39,
        56, 57, 58, 59, 60, 61, 62, 63, 48, 49, 50, 51, 52, 53, 54, 55,
        88, 73, 74, 75, 76, 77, 78, 79, 136, 65, 66, 67, 68, 69, 70, 71,
        64, 89, 90, 27, 92, 93, 94, 95, 80, 81, 82, 83, 84, 85, 86, 87,
        104, 105, 106, 107, 108, 109, 110, 111, 96, 97, 98, 99, 100, 101, 102, 103,
        120, 121, 122, 123, 124, 125, 126, 127, 112, 113, 114, 115, 116, 117, 118, 119,
        0, 137, 190, 139, 140, 141, 142, 143, 72, 129, 91, 131, 132, 133, 134, 135,
        152, 153, 154, 155, 156, 157, 158, 159, 144, 145, 146, 147, 148, 149, 150, 151,
        168, 169, 170, 171, 172, 189, 174, 175, 160, 161, 162, 163, 164, 165, 166, 167,
        184, 185, 186, 187, 188, 182, 138, 191, 176, 177, 178, 179, 180, 181, 130, 183,
        200, 173, 202, 203, 204, 205, 206, 207, 128, 193, 194, 195, 196, 197, 198, 199,
        216, 217, 218, 219, 220, 221, 222, 223, 208, 209, 210, 211, 212, 213, 214, 215,
        240, 233, 234, 235, 236, 237, 238, 247, 224, 225, 226, 227, 228, 229, 230, 231,
        248, 249, 250, 251, 252, 253, 254, 255, 232, 241, 242, 243, 244, 245, 246, 239,
    ),
    (
        8, 17, 10, 11, 12, 85, 22, 199, 0, 73, 202, 3, 4, 76, 50, 23,
        32, 41, 25, 211, 29, 13, 86, 39, 82, 9, 27, 19, 20, 37, 14, 59,
        48, 34, 42, 56, 44, 45, 30, 47, 24, 217, 33, 51, 36, 53, 38, 31,
        40, 77, 58, 15, 60, 63, 62, 119, 28, 49, 57, 35, 52, 125, 54, 55,
        72, 81, 90, 75, 71, 121, 78, 79, 64, 129, 66, 67, 157, 69, 70, 7,
        96, 89, 2, 91, 213, 93, 94, 95, 16, 88, 154, 83, 84, 92, 5, 87,
        161, 99, 106, 43, 108, 109, 110, 111, 107, 120, 98, 163, 100, 101, 102, 103,
        176, 177, 122, 123, 124, 61, 126, 191, 112, 113, 186, 115, 116, 117, 118, 74,
        136, 65, 138, 139, 68, 140, 142, 143, 128, 194, 130, 131, 196, 132, 141, 135,
        152, 208, 178, 155, 220, 230, 158, 150, 80, 145, 105, 147, 212, 156, 159, 148,
        168, 169, 170, 171, 172, 173, 174, 175, 104, 153, 162, 235, 164, 165, 166, 167,
        184, 133, 114, 187, 188, 189, 190, 127, 160, 134, 185, 179, 180, 181, 182, 183,
        200, 201, 1, 203, 204, 249, 206, 207, 192, 193, 137, 195, 205, 6, 198, 234,
        224, 144, 226, 18, 151, 253, 222, 231, 218, 209, 26, 146, 221, 21, 214, 215,
        232, 241, 210, 219, 236, 237, 246, 239, 216, 97, 250, 227, 228, 229, 46, 223,
        248, 197, 243, 251, 252, 149, 255, 254, 240, 233, 242, 225, 244, 245, 238, 247,
    ),
    (
        8, 253, 18, 11, 113, 21, 15, 4, 0, 1, 66, 19, 236, 69, 6, 248,
        32, 33, 26, 27, 12, 93, 38, 31, 16, 81, 10, 24, 220, 13, 109, 223,
        48, 41, 99, 43, 39, 36, 46, 55, 96, 25, 98, 227, 228, 53, 30, 143,
        56, 57, 22, 59, 244, 101, 45, 63, 40, 49, 50, 51, 229, 125, 54, 47,
        72, 73, 130, 119, 76, 142, 14, 79, 64, 65, 9, 62, 68, 141, 42, 71,
        88, 17, 90, 91, 92, 221, 94, 174, 152, 105, 82, 83, 84, 85, 86, 111,
        89, 153, 106, 80, 108, 103, 37, 172, 161, 145, 34, 235, 100, 117, 102, 95,
        60, 78, 122, 123, 252, 180, 110, 127, 133, 77, 114, 115, 75, 181, 118, 3,
        116, 137, 146, 139, 120, 169, 132, 112, 67, 74, 194, 128, 196, 205, 158, 134,
        209, 129, 147, 226, 140, 157, 166, 159, 144, 121, 168, 154, 28, 149, 150, 151,
        155, 104, 170, 162, 156, 173, 70, 175, 136, 97, 135, 163, 20, 165, 198, 167,
        184, 204, 186, 171, 188, 189, 138, 191, 176, 177, 185, 178, 131, 190, 182, 183,
        208, 201, 202, 203, 7, 5, 206, 215, 192, 193, 2, 195, 249, 197, 214, 199,
        160, 225, 218, 216, 148, 61, 230, 87, 200, 210, 219, 211, 213, 212, 126, 207,
        240, 241, 242, 107, 29, 245, 238, 23, 224, 217, 58, 35, 44, 239, 222, 231,
        232, 233, 187, 179, 164, 124, 254, 255, 251, 250, 234, 243, 52, 237, 246, 247,
    ),
    (
        3, 9, 47, 19, 20, 237, 248, 23, 40, 1, 253, 115, 108, 22, 30, 7,
        24, 42, 34, 0, 28, 37, 230, 223, 25, 217, 33, 11, 12, 21, 246, 4,
        16, 49, 35, 91, 52, 53, 54, 239, 32, 232, 26, 51, 228, 29, 238, 245,
        64, 57, 58, 31, 60, 61, 62, 71, 43, 41, 50, 48, 36, 45, 46, 127,
        72, 129, 74, 75, 76, 77, 78, 135, 56, 65, 66, 67, 68, 69, 70, 63,
        96, 89, 146, 59, 92, 94, 84, 118, 80, 81, 82, 131, 85, 117, 93, 87,
        104, 105, 90, 107, 44, 109, 110, 158, 88, 97, 98, 99, 164, 101, 111, 102,
        120, 121, 171, 114, 124, 125, 126, 95, 112, 224, 186, 79, 180, 73, 119, 183,
        137, 130, 182, 83, 140, 134, 142, 143, 128, 166, 155, 203, 132, 133, 178, 148,
        152, 241, 138, 8, 156, 141, 157, 86, 136, 17, 153, 147, 150, 213, 167, 163,
        161, 169, 106, 168, 172, 149, 159, 175, 160, 233, 162, 144, 188, 195, 173, 103,
        192, 185, 122, 187, 247, 189, 190, 199, 176, 177, 170, 179, 116, 181, 174, 139,
        200, 209, 202, 211, 204, 205, 214, 207, 184, 193, 194, 27, 196, 197, 198, 191,
        145, 208, 226, 154, 231, 229, 220, 151, 249, 201, 210, 255, 212, 165, 206, 215,
        227, 234, 225, 243, 244, 38, 222, 39, 10, 250, 218, 219, 254, 221, 252, 2,
        15, 251, 240, 123, 100, 18, 6, 55, 216, 13, 113, 235, 236, 5, 14, 242,
    ),
    (
        218, 54, 23, 19, 20, 30, 241, 15, 208, 61, 18, 63, 4, 5, 21, 47,
        211, 225, 234, 35, 36, 29, 13, 192, 8, 10, 14, 11, 12, 7, 6, 2,
        40, 209, 50, 16, 200, 53, 46, 231, 43, 221, 41, 27, 28, 37, 38, 39,
        25, 65, 51, 59, 60, 124, 70, 222, 99, 49, 42, 56, 44, 45, 118, 52,
        80, 73, 74, 75, 76, 77, 114, 87, 128, 57, 66, 139, 68, 69, 62, 71,
        88, 89, 146, 91, 92, 101, 94, 95, 72, 81, 97, 83, 84, 85, 86, 79,
        112, 48, 106, 163, 108, 125, 110, 111, 96, 98, 90, 67, 100, 117, 103, 102,
        120, 121, 58, 123, 64, 109, 189, 215, 104, 113, 78, 115, 116, 93, 127, 126,
        136, 137, 154, 130, 140, 157, 206, 171, 24, 129, 170, 131, 156, 134, 141, 135,
        152, 153, 82, 155, 212, 173, 158, 159, 144, 145, 138, 147, 148, 133, 150, 151,
        176, 169, 105, 186, 172, 149, 174, 183, 160, 161, 162, 107, 164, 165, 166, 167,
        132, 193, 122, 187, 191, 182, 198, 119, 168, 177, 178, 179, 180, 188, 181, 175,
        232, 203, 210, 55, 197, 213, 142, 143, 0, 185, 194, 195, 196, 204, 190, 184,
        224, 17, 217, 227, 228, 201, 247, 214, 1, 216, 202, 32, 199, 205, 22, 239,
        33, 34, 233, 243, 244, 9, 238, 223, 250, 26, 242, 219, 220, 246, 230, 31,
        249, 253, 251, 248, 3, 252, 226, 207, 240, 245, 229, 235, 236, 255, 237, 254,
    ),
    (
        24, 200, 18, 2, 12, 21, 34, 4, 0, 11, 218, 3, 20, 14, 5, 248,
        80, 208, 39, 35, 36, 15, 30, 7, 193, 17, 10, 19, 31, 13, 6, 23,
        168, 240, 238, 51, 52, 9, 54, 45, 8, 1, 210, 27, 28, 16, 50, 223,
        59, 57, 66, 115, 116, 69, 183, 63, 48, 217, 38, 43, 44, 124, 37, 55,
        75, 81, 67, 147, 156, 68, 86, 79, 60, 65, 58, 64, 148, 61, 71, 76,
        96, 89, 90, 91, 87, 93, 101, 103, 140, 73, 74, 82, 85, 77, 78, 92,
        104, 105, 106, 32, 108, 165, 94, 111, 88, 97, 98, 83, 100, 110, 102, 95,
        120, 121, 122, 99, 117, 129, 126, 127, 112, 113, 114, 70, 72, 181, 118, 119,
        136, 138, 190, 195, 176, 141, 142, 143, 128, 131, 130, 137, 196, 185, 134, 135,
        160, 153, 154, 179, 173, 157, 158, 167, 144, 145, 146, 163, 84, 149, 150, 151,
        123, 177, 170, 171, 172, 166, 182, 175, 152, 161, 178, 107, 164, 125, 109, 159,
        184, 56, 194, 187, 155, 197, 191, 254, 40, 169, 133, 162, 180, 188, 174, 46,
        209, 201, 62, 211, 212, 49, 207, 198, 192, 53, 186, 139, 132, 189, 214, 199,
        226, 216, 202, 227, 228, 225, 205, 47, 41, 42, 25, 203, 204, 213, 230, 239,
        249, 33, 242, 235, 229, 245, 222, 246, 233, 224, 206, 219, 220, 29, 22, 215,
        241, 221, 250, 251, 252, 253, 255, 236, 232, 247, 234, 243, 244, 237, 231, 26,
    ),
    (
        45, 17, 10, 2, 232, 13, 22, 250, 32, 39, 38, 227, 249, 7, 6, 239,
        209, 50, 34, 25, 12, 37, 31, 15, 56, 9, 27, 11, 5, 237, 14, 248,
        184, 41, 206, 51, 52, 33, 30, 36, 57, 197, 26, 35, 3, 29, 42, 255,
        58, 40, 49, 67, 68, 214, 55, 65, 16, 186, 69, 43, 44, 253, 169, 0,
        72, 73, 82, 131, 71, 85, 78, 84, 75, 117, 63, 59, 60, 64, 70, 87,
        88, 97, 154, 103, 93, 157, 102, 95, 152, 81, 74, 96, 175, 77, 118, 79,
        112, 122, 105, 107, 108, 109, 110, 119, 98, 89, 162, 99, 116, 125, 94, 100,
        120, 121, 48, 123, 124, 66, 126, 127, 104, 113, 185, 83, 147, 164, 90, 111,
        144, 137, 138, 201, 140, 141, 142, 151, 128, 129, 130, 190, 132, 133, 134, 135,
        146, 161, 91, 155, 213, 114, 166, 159, 136, 106, 145, 139, 189, 92, 149, 143,
        168, 171, 178, 148, 180, 181, 172, 150, 160, 153, 163, 179, 165, 101, 158, 167,
        177, 156, 202, 195, 196, 86, 174, 191, 76, 176, 170, 115, 80, 173, 62, 183,
        200, 192, 61, 211, 212, 8, 205, 207, 193, 194, 53, 187, 188, 54, 235, 199,
        219, 24, 226, 1, 244, 229, 182, 251, 215, 225, 208, 203, 204, 220, 223, 46,
        210, 241, 18, 242, 28, 231, 246, 47, 216, 230, 218, 217, 19, 221, 222, 198,
        224, 4, 234, 240, 247, 228, 21, 236, 20, 233, 23, 243, 254, 245, 238, 252,
    ),
    (
        16, 252, 254, 12, 9, 212, 235, 23, 10, 203, 42, 242, 196, 6, 18, 30,
        52, 33, 11, 227, 236, 2, 38, 36, 216, 17, 14, 248, 31, 20, 28, 29,
        224, 201, 50, 27, 45, 53, 54, 15, 32, 193, 210, 13, 241, 253, 231, 39,
        56, 198, 49, 67, 68, 76, 190, 63, 48, 170, 178, 234, 3, 25, 22, 191,
        159, 24, 74, 83, 84, 85, 78, 69, 88, 164, 182, 219, 51, 61, 70, 92,
        58, 89, 98, 152, 108, 101, 179, 95, 72, 81, 80, 19, 115, 86, 66, 87,
        40, 113, 106, 104, 167, 109, 118, 124, 96, 97, 99, 55, 116, 110, 100, 103,
        128, 121, 122, 123, 102, 125, 126, 135, 160, 105, 114, 79, 73, 117, 119, 111,
        155, 145, 138, 139, 140, 141, 133, 207, 120, 129, 130, 131, 132, 165, 134, 127,
        168, 153, 136, 112, 156, 150, 158, 199, 144, 137, 146, 163, 148, 149, 142, 151,
        161, 185, 147, 169, 181, 82, 175, 166, 176, 226, 154, 107, 143, 157, 94, 183,
        162, 93, 77, 250, 228, 189, 71, 90, 237, 177, 174, 171, 172, 75, 62, 173,
        200, 194, 238, 1, 0, 249, 218, 91, 192, 65, 186, 187, 188, 57, 184, 223,
        34, 233, 255, 195, 244, 7, 243, 214, 208, 209, 202, 41, 229, 205, 180, 215,
        204, 245, 8, 35, 251, 37, 47, 220, 197, 217, 206, 64, 213, 46, 222, 230,
        4, 225, 240, 59, 60, 21, 247, 221, 232, 211, 26, 43, 5, 246, 44, 239,
    ),
    (
        1, 0, 11, 195, 50, 246, 4, 235, 202, 8, 42, 45, 196, 12, 120, 137,
        32, 211, 218, 36, 34, 197, 28, 39, 51, 191, 30, 219, 226, 101, 31, 55,
        24, 49, 240, 29, 179, 52, 54, 47, 153, 33, 228, 59, 60, 25, 96, 37,
        76, 118, 66, 15, 230, 69, 62, 148, 87, 71, 80, 229, 245, 233, 190, 106,
        225, 107, 102, 83, 84, 57, 90, 27, 136, 177, 67, 203, 7, 174, 70, 199,
        20, 65, 91, 99, 100, 58, 94, 95, 109, 146, 74, 16, 68, 86, 93, 119,
        17, 40, 114, 123, 103, 117, 22, 6, 88, 89, 98, 178, 116, 48, 108, 72,
        241, 129, 122, 79, 124, 125, 134, 222, 104, 105, 113, 115, 164, 149, 110, 111,
        144, 145, 131, 192, 127, 132, 78, 151, 217, 121, 130, 183, 176, 133, 126, 220,
        128, 81, 162, 82, 204, 152, 158, 135, 210, 227, 138, 139, 140, 141, 150, 255,
        168, 97, 161, 53, 184, 166, 154, 175, 160, 38, 147, 155, 156, 157, 247, 167,
        56, 85, 77, 187, 188, 170, 165, 63, 180, 92, 173, 171, 172, 182, 200, 75,
        73, 181, 209, 44, 251, 21, 142, 143, 185, 193, 186, 64, 163, 189, 198, 215,
        224, 169, 18, 9, 213, 238, 61, 112, 208, 201, 237, 19, 205, 13, 206, 231,
        159, 41, 194, 253, 248, 23, 214, 207, 216, 221, 254, 249, 232, 252, 2, 223,
        35, 242, 234, 250, 26, 239, 236, 46, 10, 43, 5, 243, 244, 212, 3, 14,
    ),
    None,
    None,
    None,
    None,
    None,
    None,
)
COL_FILL = (
    (
        1, 9, 10, 11, 12, 13, 14, 6, 0, 8, 2, 3, 4, 5, 15, 7,
        24, 25, 26, 27, 28, 29, 30, 31, 16, 17, 18, 19, 20, 21, 22, 23,
        40, 41, 42, 43, 44, 45, 46, 47, 32, 33, 34, 35, 36, 37, 38, 39,
        56, 57, 58, 59, 60, 61, 62, 63, 48, 49, 50, 51, 52, 53, 54, 55,
        72, 73, 74, 75, 76, 77, 78, 79, 64, 65, 66, 67, 68, 69, 70, 71,
        88, 89, 90, 91, 92, 93, 94, 95, 80, 81, 82, 83, 84, 85, 86, 87,
        104, 105, 106, 107, 108, 109, 110, 111, 96, 97, 98, 99, 100, 101, 102, 103,
        120, 121, 122, 123, 124, 125, 126, 127, 112, 113, 114, 115, 116, 117, 118, 119,
        136, 137, 138, 139, 140, 141, 142, 143, 128, 129, 130, 131, 132, 133, 134, 135,
        152, 153, 154, 155, 156, 157, 158, 159, 144, 145, 146, 147, 148, 149, 150, 151,
        168, 169, 170, 171, 172, 173, 174, 175, 160, 161, 162, 163, 164, 165, 166, 167,
        184, 185, 186, 187, 188, 189, 190, 191, 176, 177, 178, 179, 180, 181, 182, 183,
        200, 201, 202, 203, 204, 205, 206, 207, 192, 193, 194, 195, 196, 197, 198, 199,
        216, 217, 218, 219, 220, 221, 222, 223, 208, 209, 210, 211, 212, 213, 214, 215,
        232, 233, 234, 235, 236, 237, 238, 239, 224, 225, 226, 227, 228, 229, 230, 231,
        248, 240, 250, 251, 252, 253, 247, 255, 249, 241, 242, 243, 244, 245, 246, 254,
    ),
    (
        8, 2, 10, 11, 12, 13, 5, 15, 0, 1, 9, 3, 4, 14, 6, 7,
        17, 25, 26, 27, 28, 29, 30, 22, 16, 24, 18, 19, 20, 21, 31, 23,
        40, 41, 42, 43, 44, 45, 46, 47, 32, 33, 34, 35, 36, 37, 38, 39,
        56, 57, 58, 59, 60, 61, 62, 63, 48, 49, 50, 51, 52, 53, 54, 55,
        72, 73, 74, 75, 76, 77, 78, 79, 64, 65, 66, 67, 68, 69, 70, 71,
        88, 89, 90, 91, 92, 93, 94, 95, 80, 81, 82, 83, 84, 85, 86, 87,
        104, 105, 106, 107, 108, 109, 110, 111, 96, 97, 98, 99, 100, 101, 102, 103,
        120, 121, 122, 123, 124, 125, 126, 127, 112, 113, 114, 115, 116, 117, 118, 119,
        136, 137, 138, 139, 140, 141, 142, 143, 128, 129, 130, 131, 132, 133, 134, 135,
        152, 153, 154, 155, 156, 157, 158, 159, 144, 145, 146, 147, 148, 149, 150, 151,
        168, 169, 170, 171, 172, 173, 174, 175, 160, 161, 162, 163, 164, 165, 166, 167,
        184, 185, 186, 187, 188, 189, 190, 191, 176, 177, 178, 179, 180, 181, 182, 183,
        200, 201, 202, 203, 204, 205, 206, 207, 192, 193, 194, 195, 196, 197, 198, 199,
        216, 217, 218, 219, 220, 221, 222, 223, 208, 209, 210, 211, 212, 213, 214, 215,
        232, 224, 234, 235, 236, 237, 231, 239, 233, 225, 226, 227, 228, 229, 230, 238,
        248, 249, 241, 251, 252, 246, 254, 255, 240, 250, 242, 243, 244, 245, 253, 247,
    ),
    (
        8, 9, 3, 11, 12, 4, 14, 15, 0, 1, 2, 10, 13, 5, 6, 7,
        24, 18, 26, 27, 28, 37, 21, 31, 16, 17, 25, 19, 20, 30, 22, 23,
        33, 41, 42, 43, 228, 45, 46, 38, 32, 40, 34, 35, 36, 44, 47, 39,
        56, 57, 58, 59, 60, 61, 62, 63, 48, 49, 50, 51, 52, 253, 54, 55,
        72, 73, 74, 75, 76, 121, 78, 79, 64, 65, 66, 67, 68, 113, 70, 71,
        88, 89, 90, 91, 92, 93, 94, 95, 80, 81, 82, 83, 84, 85, 86, 87,
        104, 105, 106, 107, 108, 109, 110, 111, 96, 97, 98, 99, 100, 101, 102, 103,
        120, 177, 122, 123, 124, 125, 126, 127, 69, 77, 114, 115, 116, 117, 118, 119,
        152, 137, 138, 139, 140, 141, 142, 187, 164, 129, 130, 131, 132, 133, 134, 135,
        145, 169, 154, 155, 156, 157, 158, 159, 144, 161, 146, 147, 148, 149, 150, 151,
        168, 160, 170, 171, 180, 173, 174, 175, 128, 153, 226, 163, 229, 165, 166, 167,
        184, 185, 186, 143, 188, 189, 190, 191, 176, 240, 178, 179, 181, 136, 182, 183,
        200, 201, 202, 203, 204, 205, 206, 207, 192, 193, 194, 195, 196, 197, 198, 199,
        216, 208, 218, 219, 220, 29, 215, 223, 217, 209, 210, 211, 212, 213, 214, 222,
        232, 233, 225, 162, 236, 230, 238, 239, 224, 234, 235, 227, 172, 221, 237, 231,
        248, 249, 250, 242, 245, 53, 254, 255, 112, 241, 251, 243, 244, 252, 246, 247,
    ),
    (
        8, 9, 10, 4, 3, 6, 22, 14, 0, 1, 30, 12, 11, 15, 242, 7,
        24, 25, 19, 219, 28, 20, 23, 31, 16, 17, 234, 26, 29, 237, 150, 5,
        40, 34, 35, 227, 44, 45, 37, 36, 32, 42, 41, 27, 47, 46, 38, 2,
        49, 57, 58, 59, 60, 61, 62, 54, 48, 56, 50, 51, 52, 53, 63, 55,
        72, 73, 74, 75, 115, 77, 78, 79, 64, 65, 66, 67, 92, 69, 70, 71,
        88, 89, 83, 91, 76, 86, 93, 159, 80, 81, 82, 43, 68, 85, 102, 87,
        104, 105, 90, 107, 108, 109, 111, 95, 96, 97, 98, 99, 100, 101, 94, 103,
        120, 121, 106, 123, 124, 125, 126, 127, 112, 113, 114, 122, 116, 117, 118, 119,
        136, 137, 138, 139, 140, 141, 142, 143, 128, 129, 130, 167, 132, 133, 134, 135,
        152, 153, 154, 131, 156, 157, 158, 175, 144, 145, 146, 147, 148, 149, 222, 151,
        168, 169, 170, 171, 180, 173, 174, 183, 160, 161, 162, 163, 228, 165, 110, 166,
        184, 185, 186, 187, 172, 189, 190, 191, 176, 177, 178, 179, 84, 181, 182, 188,
        200, 192, 202, 203, 204, 205, 199, 207, 201, 193, 194, 195, 196, 197, 198, 206,
        216, 217, 209, 155, 220, 214, 246, 223, 233, 218, 210, 211, 212, 213, 221, 215,
        208, 33, 18, 226, 229, 238, 239, 255, 248, 225, 235, 224, 164, 236, 21, 39,
        249, 232, 250, 244, 243, 253, 254, 231, 240, 13, 241, 252, 251, 245, 230, 247,
    ),
    (
        8, 9, 10, 2, 5, 13, 14, 15, 0, 1, 11, 3, 4, 12, 6, 7,
        24, 25, 26, 20, 19, 29, 30, 31, 16, 17, 18, 28, 27, 21, 22, 23,
        40, 41, 35, 43, 44, 36, 46, 47, 32, 33, 34, 42, 45, 37, 38, 39,
        56, 50, 58, 59, 60, 61, 53, 63, 48, 49, 57, 51, 52, 62, 54, 55,
        65, 73, 74, 75, 76, 77, 78, 70, 64, 72, 66, 67, 68, 69, 79, 71,
        88, 89, 90, 91, 92, 93, 94, 95, 80, 81, 82, 83, 84, 85, 86, 87,
        104, 105, 106, 107, 108, 109, 110, 111, 96, 97, 98, 99, 100, 101, 102, 103,
        120, 121, 122, 123, 124, 125, 126, 127, 112, 113, 114, 115, 116, 117, 118, 119,
        136, 137, 138, 139, 140, 141, 142, 143, 128, 129, 130, 131, 132, 133, 134, 135,
        152, 153, 154, 155, 156, 157, 158, 159, 144, 145, 146, 147, 148, 149, 150, 151,
        168, 169, 170, 171, 172, 173, 174, 175, 160, 161, 162, 163, 164, 165, 166, 167,
        184, 176, 186, 187, 188, 189, 183, 191, 185, 177, 178, 179, 180, 181, 182, 190,
        200, 201, 193, 203, 204, 198, 206, 207, 192, 202, 194, 195, 196, 197, 205, 199,
        216, 217, 218, 210, 213, 221, 222, 223, 208, 209, 219, 211, 212, 220, 214, 215,
        232, 233, 234, 228, 227, 237, 238, 239, 224, 225, 226, 236, 235, 229, 230, 231,
        248, 249, 243, 251, 252, 244, 254, 255, 240, 241, 242, 250, 253, 245, 246, 247,
    ),
    (
        8, 9, 1, 11, 12, 6, 14, 15, 0, 10, 2, 3, 4, 5, 13, 7,
        24, 25, 26, 18, 21, 29, 30, 31, 16, 17, 27, 19, 20, 28, 22, 23,
        40, 41, 42, 36, 35, 45, 46, 47, 32, 33, 34, 44, 43, 37, 39, 38,
        56, 57, 51, 59, 60, 52, 62, 63, 48, 49, 50, 58, 61, 53, 54, 55,
        72, 66, 74, 75, 76, 77, 69, 79, 64, 65, 73, 67, 68, 78, 70, 71,
        81, 89, 90, 91, 92, 93, 94, 86, 80, 88, 82, 83, 84, 85, 95, 87,
        104, 105, 106, 107, 108, 109, 110, 111, 96, 97, 98, 99, 100, 101, 102, 103,
        120, 121, 122, 123, 124, 125, 126, 127, 112, 113, 114, 115, 116, 117, 118, 119,
        136, 137, 138, 139, 140, 141, 142, 143, 128, 129, 130, 131, 132, 133, 134, 135,
        152, 153, 154, 155, 156, 157, 158, 159, 144, 145, 146, 147, 148, 149, 150, 151,
        168, 160, 170, 171, 172, 173, 167, 175, 169, 161, 162, 163, 164, 165, 166, 174,
        184, 185, 177, 187, 188, 182, 190, 191, 176, 186, 178, 179, 180, 181, 189, 183,
        200, 201, 202, 194, 197, 205, 214, 207, 192, 193, 203, 195, 196, 204, 198, 199,
        216, 217, 218, 212, 211, 221, 222, 223, 208, 209, 210, 220, 219, 213, 206, 215,
        232, 233, 227, 235, 236, 228, 238, 239, 224, 225, 226, 234, 237, 229, 230, 231,
        248, 242, 250, 251, 252, 253, 245, 255, 240, 241, 249, 243, 244, 254, 246, 247,
    ),
    (
        54, 0, 39, 11, 220, 6, 7, 42, 9, 10, 2, 27, 28, 5, 249, 14,
        8, 25, 17, 216, 236, 22, 213, 15, 19, 26, 18, 251, 21, 30, 29, 13,
        208, 41, 32, 34, 37, 46, 194, 36, 33, 65, 43, 35, 252, 44, 38, 31,
        56, 57, 58, 52, 51, 61, 62, 63, 48, 24, 186, 60, 59, 53, 202, 55,
        72, 73, 67, 75, 79, 68, 78, 69, 64, 66, 182, 74, 77, 49, 70, 132,
        88, 82, 90, 91, 95, 93, 85, 92, 80, 81, 89, 83, 84, 94, 87, 71,
        97, 105, 106, 107, 108, 109, 110, 102, 96, 104, 98, 99, 100, 101, 111, 103,
        120, 121, 122, 123, 124, 125, 126, 127, 112, 113, 114, 115, 116, 117, 118, 119,
        136, 137, 138, 139, 140, 141, 142, 143, 128, 129, 130, 131, 76, 133, 134, 135,
        152, 144, 154, 155, 156, 157, 151, 159, 153, 145, 146, 147, 148, 149, 150, 158,
        168, 169, 161, 171, 172, 166, 86, 175, 160, 170, 162, 163, 164, 165, 173, 167,
        184, 185, 50, 178, 181, 174, 190, 191, 176, 177, 187, 179, 180, 188, 222, 183,
        200, 201, 254, 196, 195, 205, 206, 207, 192, 193, 189, 204, 203, 197, 243, 199,
        240, 214, 211, 1, 12, 212, 215, 223, 209, 16, 219, 218, 221, 4, 250, 231,
        40, 226, 225, 235, 237, 239, 229, 47, 217, 234, 233, 232, 20, 238, 230, 247,
        241, 242, 210, 244, 228, 45, 253, 246, 227, 248, 198, 224, 3, 245, 255, 23,
    ),
    None,
    None,
    None,
    None,
    None,
    None,
    None,
    None,
)


def tick_pairs(n_row, n_col):
    chips = n_row // 2
    ticks = chips + n_col - 1
    rows = [[] for _ in range(ticks)]
    cols = [[] for _ in range(ticks)]
    for chip in range(chips):
        for core in range(2):
            for col in range(n_col):
                for step in (1, -1):
                    place = chip if core == 0 else chips - 1 - chip
                    place += col if step > 0 else n_col - 1 - col
                    here = (2 * chip + core) * n_col + col
                    onward = chip + 1 - 2 * core
                    if 0 <= onward < chips:
                        rows[place].append((here, (2 * onward + core) * n_col + col))
                    if 0 <= col + step < n_col:
                        cols[place].append((here, (2 * chip + core) * n_col + col + step))
    return rows[:-1], cols[:-1]


def patterns(pairs, fills):
    result = [None] * len(pairs)
    for group, fill in zip(GROUPS, fills):
        together = sorted({pair for t in group for pair in pairs[t]})
        if fill is not None:
            assert all(fill[a] == b for a, b in together)
            together = list(enumerate(fill))
        for t in group:
            result[t] = tuple(together)
    return result


def swaps(n_row, n_col):
    chip, off, even, odd = [], [], [], []
    for row in range(n_row):
        for col in range(n_col):
            here = row * n_col + col
            chip.append((here, (row ^ 1) * n_col + col))
            other = row + 1 if row % 2 else row - 1
            if 0 <= other < n_row:
                off.append((here, other * n_col + col))
            else:
                off.append((here, row * n_col + (col ^ 1)))
            even.append((here, row * n_col + (col ^ 1)))
            side = col + 1 if col % 2 else col - 1
            if 0 <= side < n_col:
                odd.append((here, row * n_col + side))
            else:
                odd.append((here, (row ^ 1) * n_col + col))
    return chip, off, even, odd


def whole(count):
    return [pl.BlockSpec(memory_space=pltpu.VMEM)] * count


def call(kernel, inputs, outputs, cost, specs=None, scratch=(), aliases=None, limit=16 << 20):
    return pl.pallas_call(
        kernel,
        out_shape=outputs,
        in_specs=specs or whole(len(inputs)),
        out_specs=jax.tree.map(lambda _: pl.BlockSpec(memory_space=pltpu.VMEM), outputs),
        scratch_shapes=list(scratch),
        input_output_aliases=aliases or {},
        cost_estimate=pl.CostEstimate(flops=cost, bytes_accessed=1 << 16, transcendentals=0),
        compiler_params=pltpu.CompilerParams(vmem_limit_bytes=limit),
    )(*inputs)


def dot(a, b):
    return jnp.dot(a, b, preferred_element_type=F32)


def span(index, width):
    if isinstance(index, int):
        return pl.ds(index * width, width)
    return pl.ds(pl.multiple_of(index * width, width), width)


def gather_kernel(side, op_ref, out_ref, sems):
    core = lax.rem(lax.axis_index("row"), 2)
    into, out = 1 - core, core
    blocks = [(into, out)]
    blocks += [(into, 3 - h) for h in range(2)]
    blocks += [(2 + h, out) for h in range(2)]
    blocks += [(2 + h, 3 - h) for h in range(2)]
    copies = []
    for n, (a, b) in enumerate(blocks):
        copies.append(
            pltpu.make_async_copy(
                op_ref.at[0, 0, span(a, side), span(b, side)], out_ref.at[n], sems.at[n]
            )
        )
    for copy in copies:
        copy.start()
    for copy in copies:
        copy.wait()


def base_kernel(chunk, forcing_ref, op_ref, held_ref, base_ref, send_ref, half_ref, sems):
    order = held_ref.shape[0]
    side = order // 4
    steps = order // chunk
    core = lax.rem(lax.axis_index("row"), 2)

    def copy(n):
        return pltpu.make_async_copy(
            op_ref.at[0, 0, span(n, chunk), :], held_ref.at[span(n, chunk), :], sems.at[n]
        )

    for n in range(steps):
        copy(n).start()
    half_ref[...] = forcing_ref[0, 0].astype(BF16)
    base_ref[...] = jnp.zeros_like(base_ref)

    def step(n, carry):
        copy(n).wait()
        base_ref[...] += dot(half_ref[:, span(n, chunk)], held_ref[span(n, chunk), :])
        return carry

    lax.fori_loop(0, steps, step, 0)
    send_ref[:, :side] = base_ref[:, span(core, side)]
    send_ref[:, side:] = base_ref[:, 2 * side :]


def place(t, n_row, n_col):
    row, col = lax.axis_index("row"), lax.axis_index("col")
    core, chip = lax.rem(row, 2), lax.div(row, 2)
    last = n_row // 2 - 1
    down = jnp.where(core == 0, chip, last - chip)
    first = down + col == t
    second = down + n_col - 1 - col == t
    head = jnp.where(second, 1, 0)
    row_edge = down == 0
    col_edge = jnp.where(second, col == n_col - 1, col == 0)
    return core, head, jnp.logical_or(first, second), row_edge, col_edge


def unless(edge, value):
    return jnp.where(edge, jnp.zeros_like(value), value)


def row_kernel(t, n_row, n_col, row_ref, col_ref, held_ref, near_ref, base_ref, far_ref, mid_ref, out_ref):
    core, head, active, row_edge, col_edge = place(t, n_row, n_col)
    loads, side = row_ref.shape

    @pl.when(active)
    def _():
        out = 1 - core
        row_in = unless(row_edge, row_ref[...])
        own = unless(col_edge, col_ref[:loads])
        value = base_ref[:, span(out, side)]
        value += dot(row_in, held_ref[span(core, side), span(out, side)])
        value += dot(own, held_ref[span(2 + head, side), span(out, side)])
        mid_ref[...] = value.astype(BF16)
        other = unless(col_edge, col_ref[loads:])
        value = far_ref[:, :side]
        value += dot(other, near_ref[3 + head])
        value += dot(mid_ref[...], near_ref[0])
        out_ref[...] = value.astype(BF16)


def col_kernel(
    t, n_row, n_col, row_ref, col_ref, mid_ref, held_ref, near_ref, base_ref, far_base_ref, *refs
):
    out_ref, own_ref, far_ref = refs[-3:]
    core, head, active, row_edge, col_edge = place(t, n_row, n_col)
    loads, side = row_ref.shape

    @pl.when(active)
    def _():
        out = 3 - head
        row_in = unless(row_edge, row_ref[...])
        own = unless(col_edge, col_ref[:loads])
        value = base_ref[:, span(out, side)]
        value += dot(row_in, held_ref[span(core, side), span(out, side)])
        value += dot(own, held_ref[span(2 + head, side), span(out, side)])
        out_ref[:loads] = value.astype(BF16)
        other = unless(col_edge, col_ref[loads:])
        value = far_base_ref[:, span(2 - head, side)]
        value += dot(mid_ref[...], near_ref[1 + head])
        value += dot(other, near_ref[5 + head])
        out_ref[loads:] = value.astype(BF16)
        own_ref[2 * head] = row_in
        own_ref[2 * head + 1] = own
        far_ref[2 * head] = mid_ref[...]
        far_ref[2 * head + 1] = other


def last_kernel(t, n_row, n_col, row_ref, col_ref, held_ref, base_ref, old_own, old_far, own_ref, far_ref):
    core, head, active, row_edge, col_edge = place(t, n_row, n_col)
    loads, side = row_ref.shape

    @pl.when(active)
    def _():
        out = 1 - core
        row_in = unless(row_edge, row_ref[...])
        own = unless(col_edge, col_ref[:loads])
        other = unless(col_edge, col_ref[loads:])
        value = base_ref[:, span(out, side)]
        value += dot(row_in, held_ref[span(core, side), span(out, side)])
        value += dot(own, held_ref[span(2 + head, side), span(out, side)])
        own_ref[2 * head] = row_in
        own_ref[2 * head + 1] = own
        far_ref[2 * head] = value.astype(BF16)
        far_ref[2 * head + 1] = other


def sum_kernel(own_ref, other_ref, held_ref, base_ref, out_ref, chip_ref, off_ref, even_ref, odd_ref, left_ref):
    core = lax.rem(lax.axis_index("row"), 2)
    parity = lax.rem(lax.axis_index("col"), 2)
    side = own_ref.shape[-1]

    def wide(ref, n):
        return ref[n].astype(F32)

    left_ref[:, span(core, side)] = ((wide(own_ref, 0) + wide(own_ref, 2)) * 0.25).astype(BF16)
    left_ref[:, span(1 - core, side)] = (
        (wide(other_ref, 0) + wide(other_ref, 2)) * 0.25
    ).astype(BF16)
    for h in range(2):
        both = wide(own_ref, 2 * h + 1) + wide(other_ref, 2 * h + 1)
        left_ref[:, span(2 + h, side)] = (both * 0.25).astype(BF16)
    for n in range(4):
        out_ref[:, span(n, side)] = base_ref[:, span(n, side)] + dot(
            left_ref[...], held_ref[:, span(n, side)]
        )
    chip_ref[...] = out_ref[:, span(1 - core, side)].astype(BF16)
    off_ref[...] = out_ref[:, span(core, side)].astype(BF16)
    even_ref[...] = out_ref[:, span(3 - parity, side)].astype(BF16)
    odd_ref[...] = out_ref[:, span(2 + parity, side)].astype(BF16)


def residual_kernel(n_row, n_col, forcing_ref, pre_ref, coupling_ref, chip_ref, off_ref, even_ref, odd_ref, pre_out, out_ref):
    row, col = lax.axis_index("row"), lax.axis_index("col")
    core, parity = lax.rem(row, 2), lax.rem(col, 2)
    side = chip_ref.shape[-1]

    def finish(index, facing):
        block = span(index, side)
        pre = pre_ref[:, block]
        pre_out[0, 0, :, block] = pre
        out_ref[0, 0, :, block] = (
            forcing_ref[0, 0, :, block] - pre + coupling_ref[:, block] * (facing - pre)
        )

    row_end = jnp.logical_or(row == 0, row == n_row - 1)
    col_end = jnp.logical_or(col == 0, col == n_col - 1)
    finish(1 - core, chip_ref[...].astype(F32))
    finish(core, unless(row_end, off_ref[...].astype(F32)))
    finish(3 - parity, even_ref[...].astype(F32))
    finish(2 + parity, unless(col_end, odd_ref[...].astype(F32)))


def local(n_row, n_col, forcing, local_op, material, stiffness):
    loads, order = forcing.shape[2:]
    side = order // 4
    chunk = side
    chip_swap, off_swap, even_swap, odd_swap = swaps(n_row, n_col)
    row_pairs, col_pairs = tick_pairs(n_row, n_col)
    row_sets = patterns(row_pairs, ROW_FILL)
    col_sets = patterns(col_pairs, COL_FILL)

    def vmem(shape, dtype):
        return pltpu.VMEM(shape, dtype)

    def shift(value, pairs):
        return lax.ppermute(value, AXES, pairs)

    anywhere = pl.BlockSpec(memory_space=pltpu.HBM)
    local_op = pltpu.with_memory_space_constraint(local_op, pltpu.HBM)
    parcel = call(
        functools.partial(gather_kernel, side),
        (local_op,),
        vmem((7, side, side), BF16),
        1 << 20,
        specs=[anywhere],
        scratch=[pltpu.SemaphoreType.DMA((7,))],
    )
    near = shift(parcel, chip_swap)
    held, base, base_parcel = call(
        functools.partial(base_kernel, chunk),
        (forcing, local_op),
        (
            vmem((order, order), BF16),
            vmem((loads, order), F32),
            vmem((loads, 3 * side), F32),
        ),
        2 * loads * order * order,
        specs=[pl.BlockSpec(memory_space=pltpu.VMEM), anywhere],
        scratch=[pltpu.VMEM((loads, order), BF16), pltpu.SemaphoreType.DMA((order // chunk,))],
    )
    far = shift(base_parcel, chip_swap)
    classes = jnp.arange(stiffness.shape[0], dtype=jnp.int32)
    coupling = jnp.sum(
        jnp.where(material[0, 0][None, :] == classes[:, None], stiffness[:, None], 0.0), axis=0
    )[None, :]

    row_in = jnp.zeros((loads, side), BF16)
    col_in = jnp.zeros((2 * loads, side), BF16)
    kept = ()
    steps = len(row_sets)
    work = 8 * loads * side * side
    traces = (vmem((4, loads, side), BF16),) * 2
    for t in range(steps):
        mid, row_out = call(
            functools.partial(row_kernel, t, n_row, n_col),
            (row_in, col_in, held, near, base, far),
            (vmem((loads, side), BF16), vmem((loads, side), BF16)),
            work,
        )
        row_next = shift(row_out, row_sets[t])
        col_out, *kept = call(
            functools.partial(col_kernel, t, n_row, n_col),
            (row_in, col_in, mid, held, near, base, far, *kept),
            (vmem((2 * loads, side), BF16), *traces),
            work,
            aliases={7: 1, 8: 2} if kept else None,
        )
        col_next = shift(col_out, col_sets[t])
        row_in, col_in = row_next, col_next
    own, away = call(
        functools.partial(last_kernel, steps, n_row, n_col),
        (row_in, col_in, held, base, *kept),
        traces,
        work,
        aliases={4: 0, 5: 1},
    )
    other = shift(away, chip_swap)
    trace = vmem((loads, side), BF16)
    pre, chip, off, even, odd = call(
        sum_kernel,
        (own, other, held, base),
        (vmem((loads, order), F32), trace, trace, trace, trace),
        2 * loads * order * order,
        scratch=[pltpu.VMEM((loads, order), BF16)],
    )
    odd = shift(odd, odd_swap)
    off = shift(off, off_swap)
    even = shift(even, even_swap)
    chip = shift(chip, chip_swap)
    arrived = (chip, off, even, odd)
    shape = jax.ShapeDtypeStruct((1, 1, loads, order), F32)
    return tuple(
        call(
            functools.partial(residual_kernel, n_row, n_col),
            (forcing, pre, coupling, *arrived),
            (shape, shape),
            1 << 20,
        )
    )


def solution(mesh):
    n_row, n_col = mesh.shape["row"], mesh.shape["col"]
    return jax.shard_map(
        functools.partial(local, n_row, n_col),
        mesh=mesh,
        in_specs=(
            P("row", "col", None, None),
            P("row", "col", None, None),
            P("row", "col", None),
            P(),
        ),
        out_specs=(P("row", "col", None, None), P("row", "col", None, None)),
        check_vma=False,
    )
```
